768 devices in a mesh: clip: 16 (over y_hi, x), frame: 48 (over y_lo, z, core).
Axes of the slice: x: 4, y: 8 (y_hi: 4, y_lo: 2; y = y_hi * 2 + y_lo), z: 12, core: 2. Of those that a mesh axis runs over, the one named last changes fastest.
Arguments:
- cotangent: bfloat16 [768, 192, 512], P(('clip', 'frame')), parts along dimension 0, may hold values from -6 to 6
- q_spatial: bfloat16 [768, 192, 512], P(('clip', 'frame')), parts along dimension 0, may hold values from -48 to 48
- k_spatial: bfloat16 [768, 192, 512], P(('clip', 'frame')), parts along dimension 0, may hold values from -48 to 48
- v_spatial: bfloat16 [768, 192, 512], P(('clip', 'frame')), parts along dimension 0, may hold values from -6 to 6
- q_temporal: bfloat16 [768, 192, 512], P('clip', 'frame'), parts along dimension 0, may hold values from -48 to 48
- k_temporal: bfloat16 [768, 192, 512], P('clip', 'frame'), parts along dimension 0, may hold values from -48 to 48
- v_temporal: bfloat16 [768, 192, 512], P('clip', 'frame'), parts along dimension 0, may hold values from -6 to 6
- w_qkv_spatial: bfloat16 [512, 1536], replicated, may hold values from -0.25 to 0.25
- w_out_spatial: bfloat16 [512, 512], replicated, may hold values from -0.25 to 0.25
- w_qkv_temporal: bfloat16 [512, 1536], replicated, may hold values from -0.25 to 0.25
- w_out_temporal: bfloat16 [512, 512], replicated, may hold values from -0.25 to 0.25
Outputs:
- input_grad: bfloat16 [768, 192, 512], P(('clip', 'frame')), parts along dimension 0
- grad_out_spatial: float32 [8192, 512], P('clip'), parts along dimension 0
- grad_out_temporal: float32 [8192, 512], P('clip'), parts along dimension 0
The draws below stay inside these ranges and needn't reach their ends.
There are 16 independent parts, one for each index of `clip`. The reference program is written for one: setup_inputs(seed, part) draws one part's arguments, and reference() takes and returns one part's arrays. A program takes and returns all parts, laid end to end along the dimension named above; an argument that names none is the same for every part. Nothing has to cross between parts.
All inputs are finite; a program needn't handle non-finite values.
Results may differ from the reference program's by a relative error of at most 0.0079.
Values may be sent and summed in bfloat16 or wider, within the bound.
No kernel may reach another device: no remote copies, remote signals or barrier semaphores. Data moves between devices by JAX's collectives and lax.ppermute only.
A program may use at most 32 MiB of HBM per device.

```python
import math
import jax
import jax.numpy as jnp
from jax import lax

D = 512
HEADS = 8
FRAMES = 48
PATCHES = 192


def drawn_pair(key, salt):
    first, second = jax.random.split(jax.random.fold_in(key, salt), 2)
    shape = (FRAMES, PATCHES, D)
    queries = jax.random.normal(first, shape, jnp.float32)
    key_rows = jax.random.normal(second, shape, jnp.float32)
    return (queries, key_rows)


def draw_q_spatial(key, part):
    return drawn_pair(key, 101)[0].astype(jnp.bfloat16)


def draw_k_spatial(key, part):
    return drawn_pair(key, 101)[1].astype(jnp.bfloat16)


def draw_q_temporal(key, part):
    return drawn_pair(key, 202)[0].astype(jnp.bfloat16)


def draw_k_temporal(key, part):
    return drawn_pair(key, 202)[1].astype(jnp.bfloat16)


def level_of(rng, dims, cuts, least, high):
    loudness = 1.0
    for dim, blocks in cuts:
        steps = jax.random.uniform(jax.random.fold_in(jax.random.fold_in(rng, 6), dim), (blocks,), jnp.float32, least / len(cuts), high / len(cuts))
        loudness = loudness * jnp.repeat(jnp.exp(steps), dims[dim] // blocks).reshape((-1,) + (1,) * (len(dims) - 1 - dim))
    return loudness


def normal_values(key, extent, spread, reach, shards=(), dtype=jnp.bfloat16):
    level = level_of(key, extent, shards, -0.22, 0.18) if shards else 1.0
    drawn = jax.random.normal(key, extent, jnp.float32) * spread * level
    return jnp.minimum(jnp.maximum(drawn, -reach), reach).astype(dtype)


def setup_inputs(seed: int = 0, part: int = 0) -> dict:
    seeds = jax.random.split(jax.random.key(seed), 12)
    own_keys = jax.random.split(jax.random.fold_in(seeds[11], part), 12)
    return {
        "cotangent": normal_values(own_keys[0], (FRAMES, PATCHES, D), 1.0, 6.0, ((0, 48),)),
        "q_spatial": draw_q_spatial(jax.random.fold_in(jax.random.fold_in(seeds[11], part), 71), part),
        "k_spatial": draw_k_spatial(jax.random.fold_in(jax.random.fold_in(seeds[11], part), 71), part),
        "v_spatial": normal_values(own_keys[3], (FRAMES, PATCHES, D), 1.0, 6.0, ((0, 48),)),
        "q_temporal": draw_q_temporal(jax.random.fold_in(jax.random.fold_in(seeds[11], part), 71), part),
        "k_temporal": draw_k_temporal(jax.random.fold_in(jax.random.fold_in(seeds[11], part), 71), part),
        "v_temporal": normal_values(own_keys[6], (FRAMES, PATCHES, D), 1.0, 6.0, ((1, 48),)),
        "w_qkv_spatial": normal_values(seeds[7], (D, 3 * D), D ** -0.5, 0.25),
        "w_out_spatial": normal_values(seeds[8], (D, D), D ** -0.5, 0.25),
        "w_qkv_temporal": normal_values(seeds[9], (D, 3 * D), D ** -0.5, 0.25),
        "w_out_temporal": normal_values(seeds[10], (D, D), D ** -0.5, 0.25),
    }


def contract_last(left_side, right_side):
    return lax.dot_general(left_side, right_side, (((1,), (1,)), ((), ())), preferred_element_type=jnp.float32)

def heads_view(array):
    return array.reshape(array.shape[:-1] + (HEADS, D // HEADS))

def attention_back(query_rows, key_rows, value_rows, upstream, score_scale, temporal):
    side_q = 'qbhd' if temporal else 'bqhd'
    side_k = 'kbhd' if temporal else 'bkhd'
    query_f = query_rows.astype(jnp.float32)
    key_f = key_rows.astype(jnp.float32)
    value_f = value_rows.astype(jnp.float32)
    upstream_f = upstream.astype(jnp.float32)
    scores = jnp.einsum(side_q + ',' + side_k + '->bhqk', query_f, key_f) * score_scale
    probs = jax.nn.softmax(scores, axis=-1)
    probs_half = probs.astype(jnp.bfloat16)
    mixed = jnp.einsum('bhqk,' + side_k + '->' + side_q, probs_half.astype(jnp.float32), value_f).astype(jnp.bfloat16)
    d_probs = jnp.einsum(side_q + ',' + side_k + '->bhqk', upstream_f, value_f)
    d_scores = (probs * (d_probs - lax.optimization_barrier(jnp.sum(probs * d_probs, axis=-1, keepdims=True))) * score_scale).astype(jnp.bfloat16)
    grad_query = jnp.einsum('bhqk,' + side_k + '->' + side_q, d_scores.astype(jnp.float32), key_f).astype(jnp.bfloat16)
    grad_key = jnp.einsum('bhqk,' + side_q + '->' + side_k, d_scores.astype(jnp.float32), query_f).astype(jnp.bfloat16)
    grad_value = jnp.einsum('bhqk,' + side_q + '->' + side_k, probs_half.astype(jnp.float32), upstream_f).astype(jnp.bfloat16)
    return (mixed, grad_query, grad_key, grad_value)

def project_back(base_rows, cotangent_parts, weights):
    summed = base_rows.astype(jnp.float32)
    for position in range(3):
        summed = summed + contract_last(cotangent_parts[position], weights[:, position * D:(position + 1) * D])
    return summed

def reference(cotangent, q_spatial, k_spatial, v_spatial, q_temporal, k_temporal, v_temporal, w_qkv_spatial, w_out_spatial, w_qkv_temporal, w_out_temporal):
    score_scale = 1.0 / math.sqrt(D // HEADS)
    flat_rows = cotangent.reshape(-1, D)
    d_mixed = contract_last(flat_rows, w_out_spatial).astype(jnp.bfloat16)
    blocks = FRAMES // 8
    stacked = tuple((array.reshape(blocks, 8, PATCHES, D) for array in (q_spatial, k_spatial, v_spatial, d_mixed.reshape(FRAMES, PATCHES, D))))

    def per_block(items):
        return attention_back(heads_view(items[0]), heads_view(items[1]), heads_view(items[2]), heads_view(items[3]), score_scale, False)
    results = lax.map(per_block, stacked)
    mixed_s, grad_q, grad_k, grad_v = [array.reshape(-1, D) for array in results]
    grad_spatial = jnp.dot(mixed_s.T, flat_rows, preferred_element_type=jnp.float32)
    inner_grad = project_back(flat_rows, (grad_q, grad_k, grad_v), w_qkv_spatial).astype(jnp.bfloat16)
    d_mixed_t = contract_last(inner_grad, w_out_temporal).astype(jnp.bfloat16)
    temporal_out = attention_back(heads_view(q_temporal), heads_view(k_temporal), heads_view(v_temporal), heads_view(d_mixed_t.reshape(FRAMES, PATCHES, D)), score_scale, True)
    mixed_t, tq, tk, tv = [array.reshape(-1, D) for array in temporal_out]
    grad_temporal = jnp.dot(mixed_t.T, inner_grad, preferred_element_type=jnp.float32)
    result = project_back(inner_grad, (tq, tk, tv), w_qkv_temporal).astype(jnp.bfloat16).reshape(FRAMES, PATCHES, D)
    grad_norm = math.sqrt(FRAMES * PATCHES)
    return (result, grad_spatial / grad_norm, grad_temporal / grad_norm)
```

```python
import functools
import math

import jax
import jax.numpy as jnp
from jax import lax
from jax.experimental import pallas as pl
from jax.experimental.pallas import tpu as pltpu
from jax.sharding import Mesh
from jax.sharding import PartitionSpec as P

D = 512
HEADS = 8
ROWS = 192
GROUP = 4
PAIR = 128
PAIRS = D // PAIR
HALF = D // 2
QUARTER = D // 4
CHIPS = 12
PIECE = 24
F32 = jnp.float32
BF16 = jnp.bfloat16
NT = (((1,), (1,)), ((), ()))
TN = (((0,), (0,)), ((), ()))
NN = (((1,), (0,)), ((), ()))
FRAME = ("frame_0", "frame_1", "frame_2")
CLIP_FRAME = ("clip", "frame_0", "frame_1", "frame_2")
SCALE = 1.0 / math.sqrt(D // HEADS)
SWAP = [(0, 1), (1, 0)]
VMEM = pl.BlockSpec(memory_space=pltpu.VMEM)
ANY = pl.BlockSpec(memory_space=pl.ANY)


def mm(a, b, dims):
    return lax.dot_general(a, b, dims, preferred_element_type=F32)


def stacked(x, low):
    zero = jnp.zeros_like(x)
    return jnp.concatenate([jnp.where(low, x, zero), jnp.where(low, zero, x)], axis=0)


def joined(x, low):
    return jnp.where(low, x[:ROWS], x[ROWS:])


def softmax_rows(scores, same):
    if same is not None:
        scores = jnp.where(same, scores, -1e30)
    shifted = jnp.exp(scores - jnp.max(scores, axis=-1, keepdims=True))
    return shifted * (1.0 / jnp.sum(shifted, axis=-1, keepdims=True))


def low_lanes():
    return lax.broadcasted_iota(jnp.int32, (ROWS, PAIR), 1) < D // HEADS


def same_patch():
    rows = lax.broadcasted_iota(jnp.int32, (2 * ROWS, ROWS), 0)
    cols = lax.broadcasted_iota(jnp.int32, (2 * ROWS, ROWS), 1)
    return jnp.bitwise_and(rows - cols, GROUP - 1) == 0


def pair_back(p, probs, q2, k, v, dm2, dqkv_ref, low):
    d_probs = mm(dm2, v, NT)
    inner = jnp.sum(probs * d_probs, axis=-1, keepdims=True)
    d_scores = (probs * (d_probs - inner)).astype(BF16)
    dqkv_ref[:, pl.ds(p * PAIR, PAIR)] = joined(mm(d_scores, k * BF16(SCALE), NN), low).astype(BF16)
    dqkv_ref[:, pl.ds(D + p * PAIR, PAIR)] = mm(d_scores, q2, TN).astype(BF16)
    dqkv_ref[:, pl.ds(2 * D + p * PAIR, PAIR)] = mm(probs.astype(BF16), dm2, TN).astype(BF16)


def spatial_kernel(x_hbm, q_hbm, k_hbm, v_hbm, wo_hbm, wqkv_hbm, out_ref, mixed_ref,
                   x_ref, q_ref, k_ref, v_ref, wo_ref, wqkv_ref, dm_ref, dqkv_ref, sems):
    pairs = ((q_hbm, q_ref), (k_hbm, k_ref), (v_hbm, v_ref), (x_hbm, x_ref), (wo_hbm, wo_ref), (wqkv_hbm, wqkv_ref))
    copies = [pltpu.make_async_copy(src, dst, sems.at[i]) for i, (src, dst) in enumerate(pairs)]
    for copy in copies:
        copy.start()
    low = low_lanes()
    for copy in copies[3:5]:
        copy.wait()
    x = x_ref[0]
    dm_ref[...] = mm(x, wo_ref[...], NT).astype(BF16)
    for copy in copies[:3]:
        copy.wait()
    for p in range(PAIRS):
        cols = pl.ds(p * PAIR, PAIR)
        q2 = stacked(q_ref[0, :, cols] * BF16(SCALE), low)
        k = k_ref[0, :, cols]
        v = v_ref[0, :, cols]
        probs = softmax_rows(mm(q2, k, NT), None)
        mixed_ref[:, cols] = joined(mm(probs.astype(BF16), v, NN), low).astype(BF16)
        pair_back(p, probs, q2, k, v, stacked(dm_ref[:, cols], low), dqkv_ref, low)
    copies[5].wait()
    out = x.astype(F32) + mm(dqkv_ref[...], wqkv_ref[...], NT)
    out_ref[...] = out.astype(BF16).reshape(ROWS // GROUP, GROUP, D)


def spatial(x, q, k, v, wo, wqkv):
    rows = pltpu.VMEM((1, ROWS, D), BF16)
    return pl.pallas_call(
        spatial_kernel,
        out_shape=(
            jax.ShapeDtypeStruct((ROWS // GROUP, GROUP, D), BF16),
            jax.ShapeDtypeStruct((ROWS, D), BF16),
        ),
        in_specs=[ANY] * 6,
        out_specs=(VMEM, VMEM),
        scratch_shapes=[rows] * 4
        + [
            pltpu.VMEM((D, D), BF16),
            pltpu.VMEM((D, 3 * D), BF16),
            pltpu.VMEM((ROWS, D), BF16),
            pltpu.VMEM((ROWS, 3 * D), BF16),
            pltpu.SemaphoreType.DMA((6,)),
        ],
        cost_estimate=pl.CostEstimate(flops=9 * 10**8, bytes_accessed=4 << 20, transcendentals=300000),
        name="spatial_back",
    )(x, q, k, v, wo, wqkv)


def flatten(refs, flat_ref):
    for i, ref in enumerate(refs):
        flat_ref[i] = ref[...].reshape(ROWS, D)


def attend_kernel(q_ref, k_ref, v_ref, mixed_ref, probs_ref, flat_ref):
    low, same = low_lanes(), same_patch()
    flatten((q_ref, k_ref, v_ref), flat_ref)
    for p in range(PAIRS):
        cols = pl.ds(p * PAIR, PAIR)
        probs = softmax_rows(mm(stacked(flat_ref[0, :, cols] * BF16(SCALE), low), flat_ref[1, :, cols], NT), same)
        probs_ref[p] = probs
        mixed_ref[:, cols] = joined(mm(probs.astype(BF16), flat_ref[2, :, cols], NN), low).astype(BF16)


def attend(q, k, v):
    return pl.pallas_call(
        attend_kernel,
        out_shape=(
            jax.ShapeDtypeStruct((ROWS, D), BF16),
            jax.ShapeDtypeStruct((PAIRS, 2 * ROWS, ROWS), F32),
        ),
        in_specs=[VMEM] * 3,
        out_specs=(VMEM, VMEM),
        scratch_shapes=[pltpu.VMEM((3, ROWS, D), BF16)],
        compiler_params=pltpu.CompilerParams(vmem_limit_bytes=16 << 20),
        cost_estimate=pl.CostEstimate(flops=2 * 10**8, bytes_accessed=2 << 20, transcendentals=300000),
        name="temporal_attend",
    )(q, k, v)


def temporal_kernel(x_ref, q_ref, k_ref, v_ref, probs_ref, wo_ref, wqkv_ref, out_ref, dm_ref, dqkv_ref, flat_ref):
    low = low_lanes()
    flatten((q_ref, k_ref, v_ref, x_ref), flat_ref)
    x = flat_ref[3]
    dm_ref[...] = mm(x, wo_ref[...], NT).astype(BF16)
    for p in range(PAIRS):
        cols = pl.ds(p * PAIR, PAIR)
        q2 = stacked(flat_ref[0, :, cols] * BF16(SCALE), low)
        dm2 = stacked(dm_ref[:, cols], low)
        pair_back(p, probs_ref[p], q2, flat_ref[1, :, cols], flat_ref[2, :, cols], dm2, dqkv_ref, low)
    out = x.astype(F32) + mm(dqkv_ref[...], wqkv_ref[...], NT)
    out_ref[...] = out.astype(BF16).reshape(ROWS // GROUP, GROUP, D)


def temporal(x, q, k, v, probs, wo, wqkv):
    return pl.pallas_call(
        temporal_kernel,
        out_shape=jax.ShapeDtypeStruct((ROWS // GROUP, GROUP, D), BF16),
        in_specs=[VMEM] * 7,
        out_specs=VMEM,
        scratch_shapes=[
            pltpu.VMEM((ROWS, D), BF16),
            pltpu.VMEM((ROWS, 3 * D), BF16),
            pltpu.VMEM((4, ROWS, D), BF16),
        ],
        compiler_params=pltpu.CompilerParams(vmem_limit_bytes=16 << 20),
        cost_estimate=pl.CostEstimate(flops=7 * 10**8, bytes_accessed=5 << 20, transcendentals=0),
        name="temporal_back",
    )(x, q, k, v, probs, wo, wqkv)


def outer_kernel(factor, core_ref, mixed_ref, x_ref, send_ref, keep_ref):
    core = core_ref[0]
    x = x_ref[...].reshape(ROWS, D)
    theirs = pl.ds(pl.multiple_of((1 - core) * HALF, HALF), HALF)
    ours = pl.ds(pl.multiple_of(core * HALF, HALF), HALF)
    send_ref[...] = (mm(mixed_ref[:, theirs], x, TN) * factor).astype(BF16)
    keep_ref[...] = mm(mixed_ref[:, ours], x, TN) * factor


def outer(mixed, x, core, factor):
    return pl.pallas_call(
        functools.partial(outer_kernel, factor),
        out_shape=(jax.ShapeDtypeStruct((HALF, D), BF16), jax.ShapeDtypeStruct((HALF, D), F32)),
        in_specs=[pl.BlockSpec(memory_space=pltpu.SMEM), VMEM, VMEM],
        out_specs=(VMEM, VMEM),
        compiler_params=pltpu.CompilerParams(vmem_limit_bytes=16 << 20),
        cost_estimate=pl.CostEstimate(flops=10**8, bytes_accessed=1 << 20, transcendentals=0),
        name="weight_grad",
    )(core, mixed, x)


def place_kernel(where_ref, own_ref, across_ref, beside_ref, far_ref, first_ref, second_ref):
    core, chip = where_ref[0], where_ref[1]
    for source, c, y in (
        (own_ref, core, chip),
        (across_ref, core, 1 - chip),
        (beside_ref, 1 - core, chip),
        (far_ref, 1 - core, 1 - chip),
    ):
        rows = pl.ds(pl.multiple_of(c * HALF + y * QUARTER, QUARTER), QUARTER)
        first_ref[rows, :] = source[0:QUARTER, :].astype(F32)
        second_ref[rows, :] = source[QUARTER : 2 * QUARTER, :].astype(F32)


def place(where, own, across, beside, far):
    shape = jax.ShapeDtypeStruct((D, D), F32)
    return pl.pallas_call(
        place_kernel,
        out_shape=(shape, shape),
        in_specs=[pl.BlockSpec(memory_space=pltpu.SMEM)] + [VMEM] * 4,
        out_specs=(VMEM, VMEM),
        compiler_params=pltpu.CompilerParams(vmem_limit_bytes=16 << 20),
        cost_estimate=pl.CostEstimate(flops=10**6, bytes_accessed=3 << 20, transcendentals=0),
        name="place",
    )(where, own, across, beside, far)


def exchanged(blocks):
    return lax.all_to_all(blocks, FRAME, 0, 0, tiled=True)


def on_device(
    cotangent,
    q_spatial,
    k_spatial,
    v_spatial,
    q_temporal,
    k_temporal,
    v_temporal,
    w_qkv_spatial,
    w_out_spatial,
    w_qkv_temporal,
    w_out_temporal,
):
    core = lax.axis_index("frame_2").astype(jnp.int32)
    chip = lax.axis_index("frame_0").astype(jnp.int32)
    core_of = core.reshape(1)
    where = jnp.stack([core, chip])
    factor = 1.0 / math.sqrt(48 * ROWS)

    def over_pair(mixed, x):
        send, keep = outer(mixed, x, core_of, factor)
        both = keep + lax.ppermute(send, "frame_2", SWAP).astype(F32)
        theirs = lax.dynamic_slice_in_dim(both, (1 - chip) * QUARTER, QUARTER, 0).astype(BF16)
        ours = lax.dynamic_slice_in_dim(both, chip * QUARTER, QUARTER, 0)
        return ours + lax.ppermute(theirs, "frame_0", SWAP).astype(F32)

    d_x1, mixed_s = spatial(cotangent, q_spatial, k_spatial, v_spatial, w_out_spatial, w_qkv_spatial)
    d_x1_t = exchanged(d_x1)
    grad_s = over_pair(mixed_s, cotangent)
    mixed_t, probs_t = attend(q_temporal, k_temporal, v_temporal)
    grad_t = over_pair(mixed_t, d_x1_t)
    pieces = jnp.concatenate([grad_s, grad_t], axis=0).astype(BF16)
    pieces = jnp.pad(pieces, ((0, CHIPS * PIECE - 2 * QUARTER), (0, 0))).reshape(CHIPS, PIECE, D)
    parts = lax.all_to_all(pieces, "frame_1", 0, 0, tiled=True)
    total = jnp.sum(parts.astype(F32), axis=0).astype(BF16)
    spread = lax.all_to_all(jnp.broadcast_to(total[None], (CHIPS, PIECE, D)), "frame_1", 0, 0, tiled=True)
    own = spread.reshape(CHIPS * PIECE, D)[: 2 * QUARTER]
    result = exchanged(temporal(d_x1_t, q_temporal, k_temporal, v_temporal, probs_t, w_out_temporal, w_qkv_temporal))
    across = lax.ppermute(own, "frame_0", SWAP)
    beside = lax.ppermute(own, "frame_2", SWAP)
    far = lax.ppermute(across, "frame_2", SWAP)
    first, second = place(where, own, across, beside, far)
    return (result.reshape(1, ROWS, D), first, second)


def solution(mesh):
    finer = Mesh(
        mesh.devices.reshape(mesh.shape["clip"], 2, 12, 2),
        ("clip", "frame_0", "frame_1", "frame_2"),
    )
    in_specs = (
        P(CLIP_FRAME, None, None),
        P(CLIP_FRAME, None, None),
        P(CLIP_FRAME, None, None),
        P(CLIP_FRAME, None, None),
        P("clip", FRAME, None),
        P("clip", FRAME, None),
        P("clip", FRAME, None),
        P(),
        P(),
        P(),
        P(),
    )
    out_specs = (P(CLIP_FRAME, None, None), P("clip", None), P("clip", None))
    return jax.shard_map(
        on_device, mesh=finer, in_specs=in_specs, out_specs=out_specs, check_vma=False
    )
```

```python
import functools
import math

import jax
import jax.numpy as jnp
from jax import lax
from jax.experimental import pallas as pl
from jax.experimental.pallas import tpu as pltpu
from jax.sharding import Mesh
from jax.sharding import PartitionSpec as P


D = 512
HEADS = 8
ROWS = 192
GROUP = 4
PAIR = 128
PAIRS = D // PAIR
HALF = D // 2
QUARTER = D // 4
CHIPS = 12
BANDS = 3
BAND = 88
LANES = 128
F32 = jnp.float32
BF16 = jnp.bfloat16
NT = (((1,), (1,)), ((), ()))
TN = (((0,), (0,)), ((), ()))
NN = (((1,), (0,)), ((), ()))
FRAME = ("frame_0", "frame_1", "frame_2")
CLIP_FRAME = ("clip", "frame_0", "frame_1", "frame_2")
SCALE = 1.0 / math.sqrt(D // HEADS)
SWAP = [(0, 1), (1, 0)]
VMEM = pl.BlockSpec(memory_space=pltpu.VMEM)
ANY = pl.BlockSpec(memory_space=pl.ANY)


def mm(a, b, dims):
    return lax.dot_general(a, b, dims, preferred_element_type=F32)


def stacked(x, low):
    zero = jnp.zeros_like(x)
    return jnp.concatenate([jnp.where(low, x, zero), jnp.where(low, zero, x)], axis=0)


def joined(x, low):
    return jnp.where(low, x[:ROWS], x[ROWS:])


def softmax_rows(scores, same):
    if same is not None:
        scores = jnp.where(same, scores, -1e30)
    shifted = jnp.exp(scores - jnp.max(scores, axis=-1, keepdims=True))
    return shifted * (1.0 / jnp.sum(shifted, axis=-1, keepdims=True))


def low_lanes():
    return lax.broadcasted_iota(jnp.int32, (ROWS, PAIR), 1) < D // HEADS


def same_patch():
    rows = lax.broadcasted_iota(jnp.int32, (2 * ROWS, ROWS), 0)
    cols = lax.broadcasted_iota(jnp.int32, (2 * ROWS, ROWS), 1)
    return jnp.bitwise_and(rows - cols, GROUP - 1) == 0


def pair_back(p, probs, q2, k, v, dm2, dqkv_ref, low):
    d_probs = mm(dm2, v, NT)
    inner = jnp.sum(probs * d_probs, axis=-1, keepdims=True)
    d_scores = (probs * (d_probs - inner)).astype(BF16)
    dqkv_ref[:, pl.ds(p * PAIR, PAIR)] = joined(mm(d_scores, k * BF16(SCALE), NN), low).astype(BF16)
    dqkv_ref[:, pl.ds(D + p * PAIR, PAIR)] = mm(d_scores, q2, TN).astype(BF16)
    dqkv_ref[:, pl.ds(2 * D + p * PAIR, PAIR)] = mm(probs.astype(BF16), dm2, TN).astype(BF16)


def spatial_kernel(x_hbm, q_hbm, k_hbm, v_hbm, wo_hbm, wqkv_hbm, out_ref, mixed_ref,
                   x_ref, q_ref, k_ref, v_ref, wo_ref, wqkv_ref, dm_ref, dqkv_ref, sems):
    pairs = ((q_hbm, q_ref), (k_hbm, k_ref), (v_hbm, v_ref), (x_hbm, x_ref), (wo_hbm, wo_ref), (wqkv_hbm, wqkv_ref))
    copies = [pltpu.make_async_copy(src, dst, sems.at[i]) for i, (src, dst) in enumerate(pairs)]
    for copy in copies:
        copy.start()
    low = low_lanes()
    for copy in copies[3:5]:
        copy.wait()
    x = x_ref[0]
    dm_ref[...] = mm(x, wo_ref[...], NT).astype(BF16)
    for copy in copies[:3]:
        copy.wait()
    for p in range(PAIRS):
        cols = pl.ds(p * PAIR, PAIR)
        q2 = stacked(q_ref[0, :, cols] * BF16(SCALE), low)
        k = k_ref[0, :, cols]
        v = v_ref[0, :, cols]
        probs = softmax_rows(mm(q2, k, NT), None)
        mixed_ref[:, cols] = joined(mm(probs.astype(BF16), v, NN), low).astype(BF16)
        pair_back(p, probs, q2, k, v, stacked(dm_ref[:, cols], low), dqkv_ref, low)
    copies[5].wait()
    out = x.astype(F32) + mm(dqkv_ref[...], wqkv_ref[...], NT)
    out_ref[...] = out.astype(BF16).reshape(ROWS // GROUP, GROUP, D)


def spatial(x, q, k, v, wo, wqkv):
    rows = pltpu.VMEM((1, ROWS, D), BF16)
    return pl.pallas_call(
        spatial_kernel,
        out_shape=(
            jax.ShapeDtypeStruct((ROWS // GROUP, GROUP, D), BF16),
            jax.ShapeDtypeStruct((ROWS, D), BF16),
        ),
        in_specs=[ANY] * 6,
        out_specs=(VMEM, VMEM),
        scratch_shapes=[rows] * 4
        + [
            pltpu.VMEM((D, D), BF16),
            pltpu.VMEM((D, 3 * D), BF16),
            pltpu.VMEM((ROWS, D), BF16),
            pltpu.VMEM((ROWS, 3 * D), BF16),
            pltpu.SemaphoreType.DMA((6,)),
        ],
        cost_estimate=pl.CostEstimate(flops=9 * 10**8, bytes_accessed=4 << 20, transcendentals=300000),
        name="spatial_back",
    )(x, q, k, v, wo, wqkv)


def flatten(refs, flat_ref):
    for i, ref in enumerate(refs):
        flat_ref[i] = ref[...].reshape(ROWS, D)


def attend_kernel(q_ref, k_ref, v_ref, mixed_ref, probs_ref, flat_ref):
    low, same = low_lanes(), same_patch()
    flatten((q_ref, k_ref, v_ref), flat_ref)
    for p in range(PAIRS):
        cols = pl.ds(p * PAIR, PAIR)
        probs = softmax_rows(mm(stacked(flat_ref[0, :, cols] * BF16(SCALE), low), flat_ref[1, :, cols], NT), same)
        probs_ref[p] = probs
        mixed_ref[:, cols] = joined(mm(probs.astype(BF16), flat_ref[2, :, cols], NN), low).astype(BF16)


def attend(q, k, v):
    return pl.pallas_call(
        attend_kernel,
        out_shape=(
            jax.ShapeDtypeStruct((ROWS, D), BF16),
            jax.ShapeDtypeStruct((PAIRS, 2 * ROWS, ROWS), F32),
        ),
        in_specs=[VMEM] * 3,
        out_specs=(VMEM, VMEM),
        scratch_shapes=[pltpu.VMEM((3, ROWS, D), BF16)],
        compiler_params=pltpu.CompilerParams(vmem_limit_bytes=16 << 20),
        cost_estimate=pl.CostEstimate(flops=2 * 10**8, bytes_accessed=2 << 20, transcendentals=300000),
        name="temporal_attend",
    )(q, k, v)


def temporal_kernel(x_ref, q_ref, k_ref, v_ref, probs_ref, wo_ref, wqkv_ref, out_ref, dm_ref, dqkv_ref, flat_ref):
    low = low_lanes()
    flatten((q_ref, k_ref, v_ref, x_ref), flat_ref)
    x = flat_ref[3]
    dm_ref[...] = mm(x, wo_ref[...], NT).astype(BF16)
    for p in range(PAIRS):
        cols = pl.ds(p * PAIR, PAIR)
        q2 = stacked(flat_ref[0, :, cols] * BF16(SCALE), low)
        dm2 = stacked(dm_ref[:, cols], low)
        pair_back(p, probs_ref[p], q2, flat_ref[1, :, cols], flat_ref[2, :, cols], dm2, dqkv_ref, low)
    out = x.astype(F32) + mm(dqkv_ref[...], wqkv_ref[...], NT)
    out_ref[...] = out.astype(BF16).reshape(ROWS // GROUP, GROUP, D)


def temporal(x, q, k, v, probs, wo, wqkv):
    return pl.pallas_call(
        temporal_kernel,
        out_shape=jax.ShapeDtypeStruct((ROWS // GROUP, GROUP, D), BF16),
        in_specs=[VMEM] * 7,
        out_specs=VMEM,
        scratch_shapes=[
            pltpu.VMEM((ROWS, D), BF16),
            pltpu.VMEM((ROWS, 3 * D), BF16),
            pltpu.VMEM((4, ROWS, D), BF16),
        ],
        cost_estimate=pl.CostEstimate(flops=7 * 10**8, bytes_accessed=5 << 20, transcendentals=0),
        name="temporal_back",
    )(x, q, k, v, probs, wo, wqkv)


def outer_kernel(factor, core_ref, mixed_ref, x_ref, send_ref, keep_ref):
    core = core_ref[0]
    x = x_ref[...].reshape(ROWS, D)
    theirs = pl.ds(pl.multiple_of((1 - core) * HALF, HALF), HALF)
    ours = pl.ds(pl.multiple_of(core * HALF, HALF), HALF)
    send_ref[...] = (mm(mixed_ref[:, theirs], x, TN) * factor).astype(BF16)
    keep_ref[...] = mm(mixed_ref[:, ours], x, TN) * factor


def outer(mixed, x, core, factor):
    return pl.pallas_call(
        functools.partial(outer_kernel, factor),
        out_shape=(jax.ShapeDtypeStruct((HALF, D), BF16), jax.ShapeDtypeStruct((HALF, D), F32)),
        in_specs=[pl.BlockSpec(memory_space=pltpu.SMEM), VMEM, VMEM],
        out_specs=(VMEM, VMEM),
        compiler_params=pltpu.CompilerParams(vmem_limit_bytes=16 << 20),
        cost_estimate=pl.CostEstimate(flops=10**8, bytes_accessed=1 << 20, transcendentals=0),
        name="weight_grad",
    )(core, mixed, x)


def fold_kernel(keep_s_ref, got_s_ref, keep_t_ref, got_t_ref, out_ref, sum_ref):
    sum_ref[0:QUARTER, :] = keep_s_ref[...] + got_s_ref[...].astype(F32)
    sum_ref[QUARTER:HALF, :] = keep_t_ref[...] + got_t_ref[...].astype(F32)
    sum_ref[HALF:, :] = jnp.zeros((BANDS * BAND - HALF, D), F32)
    for band in range(BANDS):
        for j in range(PAIRS):
            out_ref[band * PAIRS + j] = sum_ref[
                band * BAND : (band + 1) * BAND, j * LANES : (j + 1) * LANES
            ].astype(BF16)


def fold(keep_s, got_s, keep_t, got_t):
    return pl.pallas_call(
        fold_kernel,
        out_shape=jax.ShapeDtypeStruct((CHIPS, BAND, LANES), BF16),
        in_specs=[VMEM] * 4,
        out_specs=VMEM,
        scratch_shapes=[pltpu.VMEM((BANDS * BAND, D), F32)],
        compiler_params=pltpu.CompilerParams(vmem_limit_bytes=16 << 20),
        cost_estimate=pl.CostEstimate(flops=10**6, bytes_accessed=1 << 20, transcendentals=0),
        name="fold",
    )(keep_s, got_s, keep_t, got_t)


def total_kernel(parts_ref, out_ref):
    total = parts_ref[0].astype(F32)
    for i in range(1, CHIPS):
        total = total + parts_ref[i].astype(F32)
    total = total.astype(BF16)
    for i in range(CHIPS):
        out_ref[i] = total


def total_of(parts):
    return pl.pallas_call(
        total_kernel,
        out_shape=jax.ShapeDtypeStruct((CHIPS, BAND, LANES), BF16),
        in_specs=[VMEM],
        out_specs=VMEM,
        compiler_params=pltpu.CompilerParams(vmem_limit_bytes=16 << 20),
        cost_estimate=pl.CostEstimate(flops=10**6, bytes_accessed=1 << 19, transcendentals=0),
        name="total",
    )(parts)


def place_kernel(where_ref, own_ref, across_ref, beside_ref, far_ref, first_ref, second_ref):
    core, chip = where_ref[0], where_ref[1]
    for source, c, y in (
        (own_ref, core, chip),
        (across_ref, core, 1 - chip),
        (beside_ref, 1 - core, chip),
        (far_ref, 1 - core, 1 - chip),
    ):
        base = c * HALF + y * QUARTER
        for band in range(BANDS):
            for j in range(PAIRS):
                cols = pl.ds(j * LANES, LANES)
                for out_ref, start in ((first_ref, 0), (second_ref, QUARTER)):
                    low = max(band * BAND, start)
                    high = min((band + 1) * BAND, start + QUARTER)
                    if low < high:
                        rows = pl.ds(pl.multiple_of(base + low - start, 8), high - low)
                        out_ref[rows, cols] = source[
                            band * PAIRS + j, low - band * BAND : high - band * BAND, :
                        ].astype(F32)


def place(where, own, across, beside, far):
    shape = jax.ShapeDtypeStruct((D, D), F32)
    return pl.pallas_call(
        place_kernel,
        out_shape=(shape, shape),
        in_specs=[pl.BlockSpec(memory_space=pltpu.SMEM)] + [VMEM] * 4,
        out_specs=(VMEM, VMEM),
        compiler_params=pltpu.CompilerParams(vmem_limit_bytes=16 << 20),
        cost_estimate=pl.CostEstimate(flops=10**6, bytes_accessed=3 << 20, transcendentals=0),
        name="place",
    )(where, own, across, beside, far)


def exchanged(blocks):
    return lax.all_to_all(blocks, FRAME, 0, 0, tiled=True)


def on_device(
    cotangent,
    q_spatial,
    k_spatial,
    v_spatial,
    q_temporal,
    k_temporal,
    v_temporal,
    w_qkv_spatial,
    w_out_spatial,
    w_qkv_temporal,
    w_out_temporal,
):
    core = lax.axis_index("frame_2").astype(jnp.int32)
    chip = lax.axis_index("frame_0").astype(jnp.int32)
    core_of = core.reshape(1)
    where = jnp.stack([core, chip])
    factor = 1.0 / math.sqrt(48 * ROWS)

    def over_core(mixed, x):
        send, keep = outer(mixed, x, core_of, factor)
        got = lax.ppermute(send, "frame_2", SWAP)
        both = keep + got.astype(F32)
        theirs = lax.dynamic_slice_in_dim(both, (1 - chip) * QUARTER, QUARTER, 0).astype(BF16)
        ours = lax.dynamic_slice_in_dim(both, chip * QUARTER, QUARTER, 0)
        got = lax.ppermute(theirs, "frame_0", SWAP)
        return ours, got

    d_x1, mixed_s = spatial(cotangent, q_spatial, k_spatial, v_spatial, w_out_spatial, w_qkv_spatial)
    d_x1_t = exchanged(d_x1)
    mixed_t, probs_t = attend(q_temporal, k_temporal, v_temporal)
    keep_s, got_s = over_core(mixed_s, cotangent)
    keep_t, got_t = over_core(mixed_t, d_x1_t)
    pieces = fold(keep_s, got_s, keep_t, got_t)
    parts = lax.all_to_all(pieces, "frame_1", 0, 0, tiled=True)
    patch_result = temporal(
        d_x1_t, q_temporal, k_temporal, v_temporal, probs_t, w_out_temporal, w_qkv_temporal
    )
    total = total_of(parts)
    own = lax.all_to_all(total, "frame_1", 0, 0, tiled=True)
    result = exchanged(patch_result)
    across = lax.ppermute(own, "frame_0", SWAP)
    beside = lax.ppermute(own, "frame_2", SWAP)
    far = lax.ppermute(across, "frame_2", SWAP)
    first, second = place(where, own, across, beside, far)
    return (result.reshape(1, ROWS, D), first, second)


def solution(mesh):
    finer = Mesh(
        mesh.devices.reshape(mesh.shape["clip"], 2, 12, 2),
        ("clip", "frame_0", "frame_1", "frame_2"),
    )
    in_specs = (
        P(CLIP_FRAME, None, None),
        P(CLIP_FRAME, None, None),
        P(CLIP_FRAME, None, None),
        P(CLIP_FRAME, None, None),
        P("clip", FRAME, None),
        P("clip", FRAME, None),
        P("clip", FRAME, None),
        P(),
        P(),
        P(),
        P(),
    )
    out_specs = (P(CLIP_FRAME, None, None), P("clip", None), P("clip", None))
    return jax.shard_map(
        on_device, mesh=finer, in_specs=in_specs, out_specs=out_specs, check_vma=False
    )
```

```python
import functools
import math

import jax
import jax.numpy as jnp
from jax import lax
from jax.experimental import pallas as pl
from jax.experimental.pallas import tpu as pltpu
from jax.sharding import Mesh
from jax.sharding import PartitionSpec as P


D = 512
HEADS = 8
ROWS = 192
GROUP = 4
PAIR = 128
PAIRS = D // PAIR
HALF = D // 2
QUARTER = D // 4
CHIPS = 12
BANDS = 3
BAND = 88
LANES = 128
F32 = jnp.float32
BF16 = jnp.bfloat16
NT = (((1,), (1,)), ((), ()))
TN = (((0,), (0,)), ((), ()))
NN = (((1,), (0,)), ((), ()))
FRAME = ("frame_0", "frame_1", "frame_2")
CLIP_FRAME = ("clip", "frame_0", "frame_1", "frame_2")
SCALE = 1.0 / math.sqrt(D // HEADS)
SWAP = [(0, 1), (1, 0)]
VMEM = pl.BlockSpec(memory_space=pltpu.VMEM)
ANY = pl.BlockSpec(memory_space=pl.ANY)


def mm(a, b, dims):
    return lax.dot_general(a, b, dims, preferred_element_type=F32)


def stacked(x, low):
    zero = jnp.zeros_like(x)
    return jnp.concatenate([jnp.where(low, x, zero), jnp.where(low, zero, x)], axis=0)


def joined(x, low):
    return jnp.where(low, x[:ROWS], x[ROWS:])


def softmax_rows(scores, same):
    if same is not None:
        scores = jnp.where(same, scores, -1e30)
    shifted = jnp.exp(scores - jnp.max(scores, axis=-1, keepdims=True))
    return shifted * (1.0 / jnp.sum(shifted, axis=-1, keepdims=True))


def low_lanes():
    return lax.broadcasted_iota(jnp.int32, (ROWS, PAIR), 1) < D // HEADS


def same_patch():
    rows = lax.broadcasted_iota(jnp.int32, (2 * ROWS, ROWS), 0)
    cols = lax.broadcasted_iota(jnp.int32, (2 * ROWS, ROWS), 1)
    return jnp.bitwise_and(rows - cols, GROUP - 1) == 0


def pair_back(p, probs, q2, k, v, dm2, dqkv_ref, low):
    d_probs = mm(dm2, v, NT)
    inner = jnp.sum(probs * d_probs, axis=-1, keepdims=True)
    d_scores = (probs * (d_probs - inner)).astype(BF16)
    dqkv_ref[:, pl.ds(p * PAIR, PAIR)] = joined(mm(d_scores, k * BF16(SCALE), NN), low).astype(BF16)
    dqkv_ref[:, pl.ds(D + p * PAIR, PAIR)] = mm(d_scores, q2, TN).astype(BF16)
    dqkv_ref[:, pl.ds(2 * D + p * PAIR, PAIR)] = mm(probs.astype(BF16), dm2, TN).astype(BF16)


def spatial_kernel(x_hbm, q_hbm, k_hbm, v_hbm, wo_hbm, wqkv_hbm, out_ref, mixed_ref,
                   x_ref, q_ref, k_ref, v_ref, wo_ref, wqkv_ref, dm_ref, dqkv_ref, sems):
    pairs = ((x_hbm, x_ref), (wo_hbm, wo_ref), (q_hbm, q_ref), (k_hbm, k_ref), (v_hbm, v_ref), (wqkv_hbm, wqkv_ref))
    copies = [pltpu.make_async_copy(src, dst, sems.at[i]) for i, (src, dst) in enumerate(pairs)]
    for copy in copies:
        copy.start()
    low = low_lanes()
    for copy in copies[:2]:
        copy.wait()
    x = x_ref[0]
    dm_ref[...] = mm(x, wo_ref[...], NT).astype(BF16)
    for copy in copies[2:5]:
        copy.wait()
    for p in range(PAIRS):
        cols = pl.ds(p * PAIR, PAIR)
        q2 = stacked(q_ref[0, :, cols] * BF16(SCALE), low)
        k = k_ref[0, :, cols]
        v = v_ref[0, :, cols]
        probs = softmax_rows(mm(q2, k, NT), None)
        mixed_ref[:, cols] = joined(mm(probs.astype(BF16), v, NN), low).astype(BF16)
        pair_back(p, probs, q2, k, v, stacked(dm_ref[:, cols], low), dqkv_ref, low)
    copies[5].wait()
    out = x.astype(F32) + mm(dqkv_ref[...], wqkv_ref[...], NT)
    out_ref[...] = out.astype(BF16).reshape(ROWS // GROUP, GROUP, D)


def spatial(x, q, k, v, wo, wqkv):
    rows = pltpu.VMEM((1, ROWS, D), BF16)
    return pl.pallas_call(
        spatial_kernel,
        out_shape=(
            jax.ShapeDtypeStruct((ROWS // GROUP, GROUP, D), BF16),
            jax.ShapeDtypeStruct((ROWS, D), BF16),
        ),
        in_specs=[ANY] * 6,
        out_specs=(VMEM, VMEM),
        scratch_shapes=[rows] * 4
        + [
            pltpu.VMEM((D, D), BF16),
            pltpu.VMEM((D, 3 * D), BF16),
            pltpu.VMEM((ROWS, D), BF16),
            pltpu.VMEM((ROWS, 3 * D), BF16),
            pltpu.SemaphoreType.DMA((6,)),
        ],
        cost_estimate=pl.CostEstimate(flops=9 * 10**8, bytes_accessed=4 << 20, transcendentals=300000),
        name="spatial_back",
    )(x, q, k, v, wo, wqkv)


def flatten(refs, flat_ref, first=0):
    for i, ref in enumerate(refs, first):
        flat_ref[i] = ref[...].reshape(ROWS, D)


def attend_kernel(q_ref, k_ref, v_ref, mixed_ref, probs_ref, flat_ref):
    low, same = low_lanes(), same_patch()
    flatten((q_ref, k_ref, v_ref), flat_ref)
    for p in range(PAIRS):
        cols = pl.ds(p * PAIR, PAIR)
        probs = softmax_rows(mm(stacked(flat_ref[0, :, cols] * BF16(SCALE), low), flat_ref[1, :, cols], NT), same)
        probs_ref[p] = probs
        mixed_ref[:, cols] = joined(mm(probs.astype(BF16), flat_ref[2, :, cols], NN), low).astype(BF16)


def attend(q, k, v):
    return pl.pallas_call(
        attend_kernel,
        out_shape=(
            jax.ShapeDtypeStruct((ROWS, D), BF16),
            jax.ShapeDtypeStruct((PAIRS, 2 * ROWS, ROWS), F32),
        ),
        in_specs=[VMEM] * 3,
        out_specs=(VMEM, VMEM),
        scratch_shapes=[pltpu.VMEM((3, ROWS, D), BF16)],
        compiler_params=pltpu.CompilerParams(vmem_limit_bytes=16 << 20),
        cost_estimate=pl.CostEstimate(flops=2 * 10**8, bytes_accessed=2 << 20, transcendentals=300000),
        name="temporal_attend",
    )(q, k, v)


def temporal_kernel(core_ref, x_hbm, q_hbm, k_hbm, v_hbm, probs_hbm, wo_hbm, wqkv_hbm, keep_ref, send_ref,
                    x_ref, q_ref, k_ref, v_ref, probs_ref, wo_ref, wqkv_ref, dm_ref, dqkv_ref, flat_ref, sems):
    pairs = (
        (x_hbm, x_ref), (wo_hbm, wo_ref), (q_hbm, q_ref), (k_hbm, k_ref), (v_hbm, v_ref),
        (probs_hbm, probs_ref), (wqkv_hbm, wqkv_ref),
    )
    copies = [pltpu.make_async_copy(src, dst, sems.at[i]) for i, (src, dst) in enumerate(pairs)]
    for copy in copies:
        copy.start()
    low = low_lanes()
    copies[0].wait()
    flatten((x_ref,), flat_ref)
    x = flat_ref[0]
    copies[1].wait()
    dm_ref[...] = mm(x, wo_ref[...], NT).astype(BF16)
    for copy in copies[2:6]:
        copy.wait()
    flatten((q_ref, k_ref, v_ref), flat_ref, 1)
    for p in range(PAIRS):
        cols = pl.ds(p * PAIR, PAIR)
        q2 = stacked(flat_ref[1, :, cols] * BF16(SCALE), low)
        dm2 = stacked(dm_ref[:, cols], low)
        pair_back(p, probs_ref[p], q2, flat_ref[2, :, cols], flat_ref[3, :, cols], dm2, dqkv_ref, low)
    copies[6].wait()
    out = x.astype(F32) + mm(dqkv_ref[...], wqkv_ref[...], NT)
    out = out.astype(BF16).astype(F32).reshape(ROWS // 8, 8, D)
    first = core_ref[0] == 0
    keep_ref[...] = jnp.where(first, out[:, 0:4, :], out[:, 4:8, :]).astype(BF16)
    send_ref[...] = jnp.where(first, out[:, 4:8, :], out[:, 0:4, :]).astype(BF16)


def temporal(core, x, q, k, v, probs, wo, wqkv):
    rows = pltpu.VMEM((ROWS // GROUP, GROUP, D), BF16)
    half = jax.ShapeDtypeStruct((ROWS // 8, GROUP, D), BF16)
    return pl.pallas_call(
        temporal_kernel,
        out_shape=(half, half),
        in_specs=[pl.BlockSpec(memory_space=pltpu.SMEM)] + [ANY] * 7,
        out_specs=(VMEM, VMEM),
        scratch_shapes=[rows] * 4
        + [
            pltpu.VMEM((PAIRS, 2 * ROWS, ROWS), F32),
            pltpu.VMEM((D, D), BF16),
            pltpu.VMEM((D, 3 * D), BF16),
            pltpu.VMEM((ROWS, D), BF16),
            pltpu.VMEM((ROWS, 3 * D), BF16),
            pltpu.VMEM((4, ROWS, D), BF16),
            pltpu.SemaphoreType.DMA((7,)),
        ],
        cost_estimate=pl.CostEstimate(flops=7 * 10**8, bytes_accessed=5 << 20, transcendentals=0),
        name="temporal_back",
    )(core, x, q, k, v, probs, wo, wqkv)


def order_kernel(chip_ref, keep_ref, got_ref, gather_ref, send_ref):
    chip = chip_ref[0]
    ours = pl.ds(chip * CHIPS, CHIPS)
    theirs = pl.ds((1 - chip) * CHIPS, CHIPS)
    for i, source in enumerate((keep_ref, got_ref)):
        gather_ref[:, i] = source[ours]
        send_ref[:, i] = source[theirs]


def order(chip, keep, got):
    half = jax.ShapeDtypeStruct((CHIPS, 2, GROUP, D), BF16)
    return pl.pallas_call(
        order_kernel,
        out_shape=(half, half),
        in_specs=[pl.BlockSpec(memory_space=pltpu.SMEM), VMEM, VMEM],
        out_specs=(VMEM, VMEM),
        compiler_params=pltpu.CompilerParams(vmem_limit_bytes=16 << 20),
        cost_estimate=pl.CostEstimate(flops=10**5, bytes_accessed=1 << 19, transcendentals=0),
        name="order",
    )(chip, keep, got)


def collect_kernel(where_ref, blocks_ref, out_ref):
    first = where_ref[0] == 0
    chip = where_ref[1]
    for across in range(2):
        near = blocks_ref[:, 2 * across].astype(F32)
        beside = blocks_ref[:, 2 * across + 1].astype(F32)
        rows = pl.ds((chip + across - 2 * chip * across) * CHIPS, CHIPS)
        out_ref[rows, 0:4, :] = jnp.where(first, near, beside).astype(BF16)
        out_ref[rows, 4:8, :] = jnp.where(first, beside, near).astype(BF16)


def collect(where, blocks):
    return pl.pallas_call(
        collect_kernel,
        out_shape=jax.ShapeDtypeStruct((ROWS // 8, 8, D), BF16),
        in_specs=[pl.BlockSpec(memory_space=pltpu.SMEM), VMEM],
        out_specs=VMEM,
        compiler_params=pltpu.CompilerParams(vmem_limit_bytes=16 << 20),
        cost_estimate=pl.CostEstimate(flops=10**5, bytes_accessed=1 << 19, transcendentals=0),
        name="collect",
    )(where, blocks)


def outer_kernel(factor, core_ref, mixed_ref, x_ref, send_ref, keep_ref):
    core = core_ref[0]
    x = x_ref[...].reshape(ROWS, D)
    theirs = pl.ds(pl.multiple_of((1 - core) * HALF, HALF), HALF)
    ours = pl.ds(pl.multiple_of(core * HALF, HALF), HALF)
    send_ref[...] = (mm(mixed_ref[:, theirs], x, TN) * factor).astype(BF16)
    keep_ref[...] = mm(mixed_ref[:, ours], x, TN) * factor


def outer(mixed, x, core, factor):
    return pl.pallas_call(
        functools.partial(outer_kernel, factor),
        out_shape=(jax.ShapeDtypeStruct((HALF, D), BF16), jax.ShapeDtypeStruct((HALF, D), F32)),
        in_specs=[pl.BlockSpec(memory_space=pltpu.SMEM), VMEM, VMEM],
        out_specs=(VMEM, VMEM),
        compiler_params=pltpu.CompilerParams(vmem_limit_bytes=16 << 20),
        cost_estimate=pl.CostEstimate(flops=10**8, bytes_accessed=1 << 20, transcendentals=0),
        name="weight_grad",
    )(core, mixed, x)


def fold_kernel(keep_s_ref, got_s_ref, keep_t_ref, got_t_ref, out_ref, sum_ref):
    sum_ref[0:QUARTER, :] = keep_s_ref[...] + got_s_ref[...].astype(F32)
    sum_ref[QUARTER:HALF, :] = keep_t_ref[...] + got_t_ref[...].astype(F32)
    sum_ref[HALF:, :] = jnp.zeros((BANDS * BAND - HALF, D), F32)
    for band in range(BANDS):
        for j in range(PAIRS):
            out_ref[band * PAIRS + j] = sum_ref[
                band * BAND : (band + 1) * BAND, j * LANES : (j + 1) * LANES
            ].astype(BF16)


def fold(keep_s, got_s, keep_t, got_t):
    return pl.pallas_call(
        fold_kernel,
        out_shape=jax.ShapeDtypeStruct((CHIPS, BAND, LANES), BF16),
        in_specs=[VMEM] * 4,
        out_specs=VMEM,
        scratch_shapes=[pltpu.VMEM((BANDS * BAND, D), F32)],
        compiler_params=pltpu.CompilerParams(vmem_limit_bytes=16 << 20),
        cost_estimate=pl.CostEstimate(flops=10**6, bytes_accessed=1 << 20, transcendentals=0),
        name="fold",
    )(keep_s, got_s, keep_t, got_t)


def total_kernel(parts_ref, out_ref):
    total = parts_ref[0].astype(F32)
    for i in range(1, CHIPS):
        total = total + parts_ref[i].astype(F32)
    total = total.astype(BF16)
    for i in range(CHIPS):
        out_ref[i] = total


def total_of(parts):
    return pl.pallas_call(
        total_kernel,
        out_shape=jax.ShapeDtypeStruct((CHIPS, BAND, LANES), BF16),
        in_specs=[VMEM],
        out_specs=VMEM,
        compiler_params=pltpu.CompilerParams(vmem_limit_bytes=16 << 20),
        cost_estimate=pl.CostEstimate(flops=10**6, bytes_accessed=1 << 19, transcendentals=0),
        name="total",
    )(parts)


def place_kernel(beside, where_ref, *refs):
    sources, outs, buffers, sems = refs[:2], refs[-4:-2], refs[-2], refs[-1]
    core = where_ref[0]
    chip = where_ref[1]
    if beside:
        chip = 1 - chip
    copies = []
    for i, c in enumerate((core, 1 - core)):
        for band in range(BANDS):
            for j in range(PAIRS):
                for g in range(2):
                    low = max(band * BAND, g * QUARTER)
                    high = min((band + 1) * BAND, (g + 1) * QUARTER)
                    if low < high:
                        buffers[2 * i + g, low - g * QUARTER : high - g * QUARTER, j * LANES : (j + 1) * LANES] = (
                            sources[i][band * PAIRS + j, low - band * BAND : high - band * BAND, :].astype(F32)
                        )
        rows = pl.ds(pl.multiple_of(c * HALF + chip * QUARTER, QUARTER), QUARTER)
        for g in range(2):
            copy = pltpu.make_async_copy(buffers.at[2 * i + g], outs[g].at[rows], sems.at[2 * i + g])
            copy.start()
            copies.append(copy)
    for copy in copies:
        copy.wait()


def place(beside, where, near, far, *outs):
    shape = jax.ShapeDtypeStruct((D, D), F32)
    return pl.pallas_call(
        functools.partial(place_kernel, beside),
        out_shape=(shape, shape),
        in_specs=[pl.BlockSpec(memory_space=pltpu.SMEM), VMEM, VMEM] + [ANY] * len(outs),
        out_specs=(ANY, ANY),
        scratch_shapes=[pltpu.VMEM((4, QUARTER, D), F32), pltpu.SemaphoreType.DMA((4,))],
        input_output_aliases={3: 0, 4: 1} if outs else {},
        compiler_params=pltpu.CompilerParams(vmem_limit_bytes=16 << 20),
        cost_estimate=pl.CostEstimate(flops=10**6, bytes_accessed=3 << 20, transcendentals=0),
        name="place",
    )(where, near, far, *outs)


def exchanged(blocks):
    return lax.all_to_all(blocks, FRAME, 0, 0, tiled=True)


def on_device(
    cotangent,
    q_spatial,
    k_spatial,
    v_spatial,
    q_temporal,
    k_temporal,
    v_temporal,
    w_qkv_spatial,
    w_out_spatial,
    w_qkv_temporal,
    w_out_temporal,
):
    core = lax.axis_index("frame_2").astype(jnp.int32)
    chip = lax.axis_index("frame_0").astype(jnp.int32)
    core_of = core.reshape(1)
    where = jnp.stack([core, chip])
    factor = 1.0 / math.sqrt(48 * ROWS)

    def over_core(mixed, x):
        send, keep = outer(mixed, x, core_of, factor)
        got = lax.ppermute(send, "frame_2", SWAP)
        both = keep + got.astype(F32)
        theirs = lax.dynamic_slice_in_dim(both, (1 - chip) * QUARTER, QUARTER, 0).astype(BF16)
        ours = lax.dynamic_slice_in_dim(both, chip * QUARTER, QUARTER, 0)
        got = lax.ppermute(theirs, "frame_0", SWAP)
        return ours, got

    d_x1, mixed_s = spatial(cotangent, q_spatial, k_spatial, v_spatial, w_out_spatial, w_qkv_spatial)
    d_x1_t = exchanged(d_x1)
    mixed_t, probs_t = attend(q_temporal, k_temporal, v_temporal)
    keep_s, got_s = over_core(mixed_s, cotangent)
    keep_t, got_t = over_core(mixed_t, d_x1_t)
    pieces = fold(keep_s, got_s, keep_t, got_t)
    parts = lax.all_to_all(pieces, "frame_1", 0, 0, tiled=True)
    keep_r, send_r = temporal(
        core_of, d_x1_t, q_temporal, k_temporal, v_temporal, probs_t, w_out_temporal, w_qkv_temporal
    )
    got_r = lax.ppermute(send_r, "frame_2", SWAP)
    near_r, send_r = order(chip.reshape(1), keep_r, got_r)
    far_r = lax.ppermute(send_r, "frame_0", SWAP)
    total = total_of(parts)
    own = lax.all_to_all(total, "frame_1", 0, 0, tiled=True)
    blocks = jnp.concatenate([near_r, far_r], axis=1)
    blocks = lax.all_to_all(blocks, "frame_1", 0, 0, tiled=True)
    across = lax.ppermute(own, "frame_0", SWAP)
    beside = lax.ppermute(own, "frame_2", SWAP)
    far = lax.ppermute(across, "frame_2", SWAP)
    grads = place(False, where, own, beside)
    result = collect(where, blocks)
    first, second = place(True, where, across, far, *grads)
    return (result.reshape(1, ROWS, D), first, second)


def solution(mesh):
    finer = Mesh(
        mesh.devices.reshape(mesh.shape["clip"], 2, 12, 2),
        ("clip", "frame_0", "frame_1", "frame_2"),
    )
    in_specs = (
        P(CLIP_FRAME, None, None),
        P(CLIP_FRAME, None, None),
        P(CLIP_FRAME, None, None),
        P(CLIP_FRAME, None, None),
        P("clip", FRAME, None),
        P("clip", FRAME, None),
        P("clip", FRAME, None),
        P(),
        P(),
        P(),
        P(),
    )
    out_specs = (P(CLIP_FRAME, None, None), P("clip", None), P("clip", None))
    return jax.shard_map(
        on_device, mesh=finer, in_specs=in_specs, out_specs=out_specs, check_vma=False
    )
```

```python
import functools
import math

import jax
import jax.numpy as jnp
from jax import lax
from jax.experimental import pallas as pl
from jax.experimental.pallas import tpu as pltpu
from jax.sharding import Mesh
from jax.sharding import PartitionSpec as P


D = 512
HEADS = 8
ROWS = 192
GROUP = 4
PAIR = 128
PAIRS = D // PAIR
HALF = D // 2
QUARTER = D // 4
CHIPS = 12
BANDS = 3
BAND = 88
LANES = 128
F32 = jnp.float32
BF16 = jnp.bfloat16
NT = (((1,), (1,)), ((), ()))
TN = (((0,), (0,)), ((), ()))
NN = (((1,), (0,)), ((), ()))
FRAME = ("frame_0", "frame_1", "frame_2")
CLIP_FRAME = ("clip", "frame_0", "frame_1", "frame_2")
SCALE = 1.0 / math.sqrt(D // HEADS)
SWAP = [(0, 1), (1, 0)]
VMEM = pl.BlockSpec(memory_space=pltpu.VMEM)
ANY = pl.BlockSpec(memory_space=pl.ANY)


def mm(a, b, dims):
    return lax.dot_general(a, b, dims, preferred_element_type=F32)


def stacked(x, low):
    zero = jnp.zeros_like(x)
    return jnp.concatenate([jnp.where(low, x, zero), jnp.where(low, zero, x)], axis=0)


def joined(x, low):
    return jnp.where(low, x[:ROWS], x[ROWS:])


def softmax_cols(scores, same):
    if same is not None:
        scores = jnp.where(same, scores, -1e30)
    shifted = jnp.exp(scores - jnp.max(scores, axis=0, keepdims=True))
    return shifted * (1.0 / jnp.sum(shifted, axis=0, keepdims=True))


def low_lanes():
    return lax.broadcasted_iota(jnp.int32, (ROWS, PAIR), 1) < D // HEADS


def same_patch():
    rows = lax.broadcasted_iota(jnp.int32, (ROWS, 2 * ROWS), 0)
    cols = lax.broadcasted_iota(jnp.int32, (ROWS, 2 * ROWS), 1)
    return jnp.bitwise_and(rows - cols, GROUP - 1) == 0


def pair_back(p, probs, q2, k, v, dm2, dqkv_ref, low):
    d_probs = mm(v, dm2, NT)
    inner = jnp.sum(probs * d_probs, axis=0, keepdims=True)
    d_scores = (probs * (d_probs - inner)).astype(BF16)
    dqkv_ref[:, pl.ds(p * PAIR, PAIR)] = joined(mm(d_scores, k * BF16(SCALE), TN), low).astype(BF16)
    dqkv_ref[:, pl.ds(D + p * PAIR, PAIR)] = mm(d_scores, q2, NN).astype(BF16)
    dqkv_ref[:, pl.ds(2 * D + p * PAIR, PAIR)] = mm(probs.astype(BF16), dm2, NN).astype(BF16)


def spatial_kernel(x_hbm, q_hbm, k_hbm, v_hbm, wo_hbm, wqkv_hbm, out_ref, mixed_ref,
                   x_ref, q_ref, k_ref, v_ref, wo_ref, wqkv_ref, dm_ref, dqkv_ref, sems):
    pairs = ((x_hbm, x_ref), (wo_hbm, wo_ref), (q_hbm, q_ref), (k_hbm, k_ref), (v_hbm, v_ref), (wqkv_hbm, wqkv_ref))
    copies = [pltpu.make_async_copy(src, dst, sems.at[i]) for i, (src, dst) in enumerate(pairs)]
    for copy in copies:
        copy.start()
    low = low_lanes()
    for copy in copies[:2]:
        copy.wait()
    x = x_ref[0]
    dm_ref[...] = mm(x, wo_ref[...], NT).astype(BF16)
    for copy in copies[2:5]:
        copy.wait()
    for p in range(PAIRS):
        cols = pl.ds(p * PAIR, PAIR)
        q2 = stacked(q_ref[0, :, cols] * BF16(SCALE), low)
        k = k_ref[0, :, cols]
        v = v_ref[0, :, cols]
        probs = softmax_cols(mm(k, q2, NT), None)
        mixed_ref[:, cols] = joined(mm(probs.astype(BF16), v, TN), low).astype(BF16)
        pair_back(p, probs, q2, k, v, stacked(dm_ref[:, cols], low), dqkv_ref, low)
    copies[5].wait()
    out = x.astype(F32) + mm(dqkv_ref[...], wqkv_ref[...], NT)
    out_ref[...] = out.astype(BF16).reshape(ROWS // GROUP, GROUP, D)


def spatial(x, q, k, v, wo, wqkv):
    rows = pltpu.VMEM((1, ROWS, D), BF16)
    return pl.pallas_call(
        spatial_kernel,
        out_shape=(
            jax.ShapeDtypeStruct((ROWS // GROUP, GROUP, D), BF16),
            jax.ShapeDtypeStruct((ROWS, D), BF16),
        ),
        in_specs=[ANY] * 6,
        out_specs=(VMEM, VMEM),
        scratch_shapes=[rows] * 4
        + [
            pltpu.VMEM((D, D), BF16),
            pltpu.VMEM((D, 3 * D), BF16),
            pltpu.VMEM((ROWS, D), BF16),
            pltpu.VMEM((ROWS, 3 * D), BF16),
            pltpu.SemaphoreType.DMA((6,)),
        ],
        cost_estimate=pl.CostEstimate(flops=9 * 10**8, bytes_accessed=4 << 20, transcendentals=300000),
        name="spatial_back",
    )(x, q, k, v, wo, wqkv)


def flatten(refs, flat_ref, first=0):
    for i, ref in enumerate(refs, first):
        flat_ref[i] = ref[...].reshape(ROWS, D)


def attend_kernel(q_ref, k_ref, v_ref, mixed_ref, probs_ref, flat_ref):
    low, same = low_lanes(), same_patch()
    flatten((q_ref, k_ref, v_ref), flat_ref)
    for p in range(PAIRS):
        cols = pl.ds(p * PAIR, PAIR)
        probs = softmax_cols(mm(flat_ref[1, :, cols], stacked(flat_ref[0, :, cols] * BF16(SCALE), low), NT), same)
        probs_ref[p] = probs
        mixed_ref[:, cols] = joined(mm(probs.astype(BF16), flat_ref[2, :, cols], TN), low).astype(BF16)


def attend(q, k, v):
    return pl.pallas_call(
        attend_kernel,
        out_shape=(
            jax.ShapeDtypeStruct((ROWS, D), BF16),
            jax.ShapeDtypeStruct((PAIRS, ROWS, 2 * ROWS), F32),
        ),
        in_specs=[VMEM] * 3,
        out_specs=(VMEM, VMEM),
        scratch_shapes=[pltpu.VMEM((3, ROWS, D), BF16)],
        compiler_params=pltpu.CompilerParams(vmem_limit_bytes=16 << 20),
        cost_estimate=pl.CostEstimate(flops=2 * 10**8, bytes_accessed=2 << 20, transcendentals=300000),
        name="temporal_attend",
    )(q, k, v)


def temporal_kernel(core_ref, x_hbm, q_hbm, k_hbm, v_hbm, probs_hbm, wo_hbm, wqkv_hbm, keep_ref, send_ref,
                    x_ref, q_ref, k_ref, v_ref, probs_ref, wo_ref, wqkv_ref, dm_ref, dqkv_ref, flat_ref, sems):
    pairs = (
        (x_hbm, x_ref), (wo_hbm, wo_ref), (q_hbm, q_ref), (k_hbm, k_ref), (v_hbm, v_ref),
        (probs_hbm, probs_ref), (wqkv_hbm, wqkv_ref),
    )
    copies = [pltpu.make_async_copy(src, dst, sems.at[i]) for i, (src, dst) in enumerate(pairs)]
    for copy in copies:
        copy.start()
    low = low_lanes()
    copies[0].wait()
    flatten((x_ref,), flat_ref)
    x = flat_ref[0]
    copies[1].wait()
    dm_ref[...] = mm(x, wo_ref[...], NT).astype(BF16)
    for copy in copies[2:6]:
        copy.wait()
    flatten((q_ref, k_ref, v_ref), flat_ref, 1)
    for p in range(PAIRS):
        cols = pl.ds(p * PAIR, PAIR)
        q2 = stacked(flat_ref[1, :, cols] * BF16(SCALE), low)
        dm2 = stacked(dm_ref[:, cols], low)
        pair_back(p, probs_ref[p], q2, flat_ref[2, :, cols], flat_ref[3, :, cols], dm2, dqkv_ref, low)
    copies[6].wait()
    out = x.astype(F32) + mm(dqkv_ref[...], wqkv_ref[...], NT)
    out = out.astype(BF16).astype(F32).reshape(ROWS // 8, 8, D)
    first = core_ref[0] == 0
    keep_ref[...] = jnp.where(first, out[:, 0:4, :], out[:, 4:8, :]).astype(BF16)
    send_ref[...] = jnp.where(first, out[:, 4:8, :], out[:, 0:4, :]).astype(BF16)


def temporal(core, x, q, k, v, probs, wo, wqkv):
    rows = pltpu.VMEM((ROWS // GROUP, GROUP, D), BF16)
    half = jax.ShapeDtypeStruct((ROWS // 8, GROUP, D), BF16)
    return pl.pallas_call(
        temporal_kernel,
        out_shape=(half, half),
        in_specs=[pl.BlockSpec(memory_space=pltpu.SMEM)] + [ANY] * 7,
        out_specs=(VMEM, VMEM),
        scratch_shapes=[rows] * 4
        + [
            pltpu.VMEM((PAIRS, ROWS, 2 * ROWS), F32),
            pltpu.VMEM((D, D), BF16),
            pltpu.VMEM((D, 3 * D), BF16),
            pltpu.VMEM((ROWS, D), BF16),
            pltpu.VMEM((ROWS, 3 * D), BF16),
            pltpu.VMEM((4, ROWS, D), BF16),
            pltpu.SemaphoreType.DMA((7,)),
        ],
        cost_estimate=pl.CostEstimate(flops=7 * 10**8, bytes_accessed=5 << 20, transcendentals=0),
        name="temporal_back",
    )(core, x, q, k, v, probs, wo, wqkv)


def order_kernel(chip_ref, keep_ref, got_ref, gather_ref, send_ref):
    chip = chip_ref[0]
    ours = pl.ds(chip * CHIPS, CHIPS)
    theirs = pl.ds((1 - chip) * CHIPS, CHIPS)
    for i, source in enumerate((keep_ref, got_ref)):
        gather_ref[:, i] = source[ours]
        send_ref[:, i] = source[theirs]


def order(chip, keep, got):
    half = jax.ShapeDtypeStruct((CHIPS, 2, GROUP, D), BF16)
    return pl.pallas_call(
        order_kernel,
        out_shape=(half, half),
        in_specs=[pl.BlockSpec(memory_space=pltpu.SMEM), VMEM, VMEM],
        out_specs=(VMEM, VMEM),
        compiler_params=pltpu.CompilerParams(vmem_limit_bytes=16 << 20),
        cost_estimate=pl.CostEstimate(flops=10**5, bytes_accessed=1 << 19, transcendentals=0),
        name="order",
    )(chip, keep, got)


def outer_kernel(factor, core_ref, mixed_ref, x_ref, send_ref, keep_ref):
    core = core_ref[0]
    x = x_ref[...].reshape(ROWS, D)
    theirs = pl.ds(pl.multiple_of((1 - core) * HALF, HALF), HALF)
    ours = pl.ds(pl.multiple_of(core * HALF, HALF), HALF)
    send_ref[...] = (mm(mixed_ref[:, theirs], x, TN) * factor).astype(BF16)
    keep_ref[...] = mm(mixed_ref[:, ours], x, TN) * factor


def outer(mixed, x, core, factor):
    return pl.pallas_call(
        functools.partial(outer_kernel, factor),
        out_shape=(jax.ShapeDtypeStruct((HALF, D), BF16), jax.ShapeDtypeStruct((HALF, D), F32)),
        in_specs=[pl.BlockSpec(memory_space=pltpu.SMEM), VMEM, VMEM],
        out_specs=(VMEM, VMEM),
        compiler_params=pltpu.CompilerParams(vmem_limit_bytes=16 << 20),
        cost_estimate=pl.CostEstimate(flops=10**8, bytes_accessed=1 << 20, transcendentals=0),
        name="weight_grad",
    )(core, mixed, x)


def fold_kernel(keep_s_ref, got_s_ref, keep_t_ref, got_t_ref, out_ref, sum_ref):
    sum_ref[0:QUARTER, :] = keep_s_ref[...] + got_s_ref[...].astype(F32)
    sum_ref[QUARTER:HALF, :] = keep_t_ref[...] + got_t_ref[...].astype(F32)
    sum_ref[HALF:, :] = jnp.zeros((BANDS * BAND - HALF, D), F32)
    for band in range(BANDS):
        for j in range(PAIRS):
            out_ref[band * PAIRS + j] = sum_ref[
                band * BAND : (band + 1) * BAND, j * LANES : (j + 1) * LANES
            ].astype(BF16)


def fold(keep_s, got_s, keep_t, got_t):
    return pl.pallas_call(
        fold_kernel,
        out_shape=jax.ShapeDtypeStruct((CHIPS, BAND, LANES), BF16),
        in_specs=[VMEM] * 4,
        out_specs=VMEM,
        scratch_shapes=[pltpu.VMEM((BANDS * BAND, D), F32)],
        compiler_params=pltpu.CompilerParams(vmem_limit_bytes=16 << 20),
        cost_estimate=pl.CostEstimate(flops=10**6, bytes_accessed=1 << 20, transcendentals=0),
        name="fold",
    )(keep_s, got_s, keep_t, got_t)


def total_kernel(parts_ref, out_ref):
    total = parts_ref[0].astype(F32)
    for i in range(1, CHIPS):
        total = total + parts_ref[i].astype(F32)
    total = total.astype(BF16)
    for i in range(CHIPS):
        out_ref[i] = total


def total_of(parts):
    return pl.pallas_call(
        total_kernel,
        out_shape=jax.ShapeDtypeStruct((CHIPS, BAND, LANES), BF16),
        in_specs=[VMEM],
        out_specs=VMEM,
        compiler_params=pltpu.CompilerParams(vmem_limit_bytes=16 << 20),
        cost_estimate=pl.CostEstimate(flops=10**6, bytes_accessed=1 << 19, transcendentals=0),
        name="total",
    )(parts)


def place_quarter(source, c, y, outs, buffer, sems):
    for band in range(BANDS):
        for j in range(PAIRS):
            for g in range(2):
                low = max(band * BAND, g * QUARTER)
                high = min((band + 1) * BAND, (g + 1) * QUARTER)
                if low < high:
                    buffer[g, low - g * QUARTER : high - g * QUARTER, j * LANES : (j + 1) * LANES] = source[
                        band * PAIRS + j, low - band * BAND : high - band * BAND, :
                    ].astype(F32)
    rows = pl.ds(pl.multiple_of(c * HALF + y * QUARTER, QUARTER), QUARTER)
    copies = [pltpu.make_async_copy(buffer.at[g], outs[g].at[rows], sems.at[g]) for g in range(2)]
    for copy in copies:
        copy.start()
    return copies


def near_kernel(where_ref, own_ref, beside_ref, first_ref, second_ref, buffers, sems):
    core, chip = where_ref[0], where_ref[1]
    outs = (first_ref, second_ref)
    copies = place_quarter(own_ref, core, chip, outs, buffers.at[0], sems.at[0])
    copies += place_quarter(beside_ref, 1 - core, chip, outs, buffers.at[1], sems.at[1])
    for copy in copies:
        copy.wait()


def far_kernel(where_ref, across_ref, far_ref, blocks_ref, *refs):
    first_ref, second_ref, result_ref, buffers, result, sems, result_sem = refs[2:]
    core, chip = where_ref[0], where_ref[1]
    outs = (first_ref, second_ref)
    copies = place_quarter(across_ref, core, 1 - chip, outs, buffers.at[0], sems.at[0])
    copies += place_quarter(far_ref, 1 - core, 1 - chip, outs, buffers.at[1], sems.at[1])
    for across in range(2):
        near = blocks_ref[:, 2 * across].astype(F32)
        beside = blocks_ref[:, 2 * across + 1].astype(F32)
        rows = pl.ds((chip + across - 2 * chip * across) * CHIPS, CHIPS)
        result[rows, 0:4, :] = jnp.where(core == 0, near, beside).astype(BF16)
        result[rows, 4:8, :] = jnp.where(core == 0, beside, near).astype(BF16)
    copies.append(pltpu.make_async_copy(result, result_ref, result_sem))
    copies[-1].start()
    for copy in copies:
        copy.wait()


def place(where, *arrays):
    grad = jax.ShapeDtypeStruct((D, D), F32)
    rows = jax.ShapeDtypeStruct((ROWS // 8, 8, D), BF16)
    final = len(arrays) > 2
    scratch = [pltpu.VMEM((2, 2, QUARTER, D), F32)]
    if final:
        scratch.append(pltpu.VMEM((ROWS // 8, 8, D), BF16))
    scratch.append(pltpu.SemaphoreType.DMA((2, 2)))
    if final:
        scratch.append(pltpu.SemaphoreType.DMA(()))
    return pl.pallas_call(
        far_kernel if final else near_kernel,
        out_shape=(grad, grad, rows) if final else (grad, grad),
        in_specs=[pl.BlockSpec(memory_space=pltpu.SMEM)]
        + ([VMEM] * 3 + [ANY] * 2 if final else [VMEM] * 2),
        out_specs=(ANY,) * (3 if final else 2),
        scratch_shapes=scratch,
        input_output_aliases={4: 0, 5: 1} if final else {},
        compiler_params=pltpu.CompilerParams(vmem_limit_bytes=16 << 20),
        cost_estimate=pl.CostEstimate(flops=10**6, bytes_accessed=3 << 20, transcendentals=0),
        name="place_far" if final else "place_near",
    )(where, *arrays)


def exchanged(blocks):
    return lax.all_to_all(blocks, FRAME, 0, 0, tiled=True)


def on_device(
    cotangent,
    q_spatial,
    k_spatial,
    v_spatial,
    q_temporal,
    k_temporal,
    v_temporal,
    w_qkv_spatial,
    w_out_spatial,
    w_qkv_temporal,
    w_out_temporal,
):
    core = lax.axis_index("frame_2").astype(jnp.int32)
    chip = lax.axis_index("frame_0").astype(jnp.int32)
    core_of = core.reshape(1)
    where = jnp.stack([core, chip])
    factor = 1.0 / math.sqrt(48 * ROWS)

    def over_core(mixed, x):
        send, keep = outer(mixed, x, core_of, factor)
        got = lax.ppermute(send, "frame_2", SWAP)
        both = keep + got.astype(F32)
        theirs = lax.dynamic_slice_in_dim(both, (1 - chip) * QUARTER, QUARTER, 0).astype(BF16)
        ours = lax.dynamic_slice_in_dim(both, chip * QUARTER, QUARTER, 0)
        got = lax.ppermute(theirs, "frame_0", SWAP)
        return ours, got

    d_x1, mixed_s = spatial(cotangent, q_spatial, k_spatial, v_spatial, w_out_spatial, w_qkv_spatial)
    d_x1_t = exchanged(d_x1)
    mixed_t, probs_t = attend(q_temporal, k_temporal, v_temporal)
    keep_s, got_s = over_core(mixed_s, cotangent)
    keep_t, got_t = over_core(mixed_t, d_x1_t)
    pieces = fold(keep_s, got_s, keep_t, got_t)
    parts = lax.all_to_all(pieces, "frame_1", 0, 0, tiled=True)
    keep_r, send_r = temporal(
        core_of, d_x1_t, q_temporal, k_temporal, v_temporal, probs_t, w_out_temporal, w_qkv_temporal
    )
    got_r = lax.ppermute(send_r, "frame_2", SWAP)
    near_r, send_r = order(chip.reshape(1), keep_r, got_r)
    far_r = lax.ppermute(send_r, "frame_0", SWAP)
    total = total_of(parts)
    own = lax.all_to_all(total, "frame_1", 0, 0, tiled=True)
    blocks = jnp.concatenate([near_r, far_r], axis=1)
    blocks = lax.all_to_all(blocks, "frame_1", 0, 0, tiled=True)
    across = lax.ppermute(own, "frame_0", SWAP)
    beside = lax.ppermute(own, "frame_2", SWAP)
    far = lax.ppermute(across, "frame_2", SWAP)
    grads = place(where, own, beside)
    first, second, result = place(where, across, far, blocks, *grads)
    return (result.reshape(1, ROWS, D), first, second)


def solution(mesh):
    finer = Mesh(
        mesh.devices.reshape(mesh.shape["clip"], 2, 12, 2),
        ("clip", "frame_0", "frame_1", "frame_2"),
    )
    in_specs = (
        P(CLIP_FRAME, None, None),
        P(CLIP_FRAME, None, None),
        P(CLIP_FRAME, None, None),
        P(CLIP_FRAME, None, None),
        P("clip", FRAME, None),
        P("clip", FRAME, None),
        P("clip", FRAME, None),
        P(),
        P(),
        P(),
        P(),
    )
    out_specs = (P(CLIP_FRAME, None, None), P("clip", None), P("clip", None))
    return jax.shard_map(
        on_device, mesh=finer, in_specs=in_specs, out_specs=out_specs, check_vma=False
    )
```

```python
import functools
import math

import jax
import jax.numpy as jnp
from jax import lax
from jax.experimental import pallas as pl
from jax.experimental.pallas import tpu as pltpu
from jax.sharding import Mesh
from jax.sharding import PartitionSpec as P


D = 512
HEADS = 8
ROWS = 192
GROUP = 4
PAIR = 128
PAIRS = D // PAIR
HALF = D // 2
QUARTER = D // 4
CHIPS = 12
BANDS = 3
BAND = 88
LANES = 128
F32 = jnp.float32
BF16 = jnp.bfloat16
NT = (((1,), (1,)), ((), ()))
TN = (((0,), (0,)), ((), ()))
NN = (((1,), (0,)), ((), ()))
FRAME = ("frame_0", "frame_1", "frame_2")
CLIP_FRAME = ("clip", "frame_0", "frame_1", "frame_2")
SCALE = 1.0 / math.sqrt(D // HEADS)
SWAP = [(0, 1), (1, 0)]
VMEM = pl.BlockSpec(memory_space=pltpu.VMEM)
ANY = pl.BlockSpec(memory_space=pl.ANY)


def mm(a, b, dims):
    return lax.dot_general(a, b, dims, preferred_element_type=F32)


def stacked(x, low):
    zero = jnp.zeros_like(x)
    return jnp.concatenate([jnp.where(low, x, zero), jnp.where(low, zero, x)], axis=0)


def joined(x, low):
    return jnp.where(low, x[:ROWS], x[ROWS:])


def softmax_cols(scores, same):
    if same is not None:
        scores = jnp.where(same, scores, -1e30)
    shifted = jnp.exp(scores - jnp.max(scores, axis=0, keepdims=True))
    return shifted * (1.0 / jnp.sum(shifted, axis=0, keepdims=True))


def low_lanes():
    return lax.broadcasted_iota(jnp.int32, (ROWS, PAIR), 1) < D // HEADS


def same_patch():
    rows = lax.broadcasted_iota(jnp.int32, (ROWS, 2 * ROWS), 0)
    cols = lax.broadcasted_iota(jnp.int32, (ROWS, 2 * ROWS), 1)
    return jnp.bitwise_and(rows - cols, GROUP - 1) == 0


def pair_back(p, probs, q2, k, v, dm2, dqkv_ref, low):
    d_probs = mm(v, dm2, NT)
    inner = jnp.sum(probs * d_probs, axis=0, keepdims=True)
    d_scores = (probs * (d_probs - inner)).astype(BF16)
    dqkv_ref[:, pl.ds(p * PAIR, PAIR)] = joined(mm(d_scores, k * BF16(SCALE), TN), low).astype(BF16)
    dqkv_ref[:, pl.ds(D + p * PAIR, PAIR)] = mm(d_scores, q2, NN).astype(BF16)
    dqkv_ref[:, pl.ds(2 * D + p * PAIR, PAIR)] = mm(probs.astype(BF16), dm2, NN).astype(BF16)


def spatial_kernel(x_hbm, q_hbm, k_hbm, v_hbm, wo_hbm, wqkv_hbm, out_ref, mixed_ref,
                   x_ref, q_ref, k_ref, v_ref, wo_ref, wqkv_ref, dm_ref, dqkv_ref, sems):
    pairs = ((x_hbm, x_ref), (wo_hbm, wo_ref), (q_hbm, q_ref), (k_hbm, k_ref), (v_hbm, v_ref), (wqkv_hbm, wqkv_ref))
    copies = [pltpu.make_async_copy(src, dst, sems.at[i]) for i, (src, dst) in enumerate(pairs)]
    for copy in copies:
        copy.start()
    low = low_lanes()
    for copy in copies[:2]:
        copy.wait()
    x = x_ref[0]
    dm_ref[...] = mm(x, wo_ref[...], NT).astype(BF16)
    for copy in copies[2:5]:
        copy.wait()
    for p in range(PAIRS):
        cols = pl.ds(p * PAIR, PAIR)
        q2 = stacked(q_ref[0, :, cols] * BF16(SCALE), low)
        k = k_ref[0, :, cols]
        v = v_ref[0, :, cols]
        probs = softmax_cols(mm(k, q2, NT), None)
        mixed_ref[:, cols] = joined(mm(probs.astype(BF16), v, TN), low).astype(BF16)
        pair_back(p, probs, q2, k, v, stacked(dm_ref[:, cols], low), dqkv_ref, low)
    copies[5].wait()
    out = x.astype(F32) + mm(dqkv_ref[...], wqkv_ref[...], NT)
    out_ref[...] = out.astype(BF16).reshape(ROWS // GROUP, GROUP, D)


def spatial(x, q, k, v, wo, wqkv):
    rows = pltpu.VMEM((1, ROWS, D), BF16)
    return pl.pallas_call(
        spatial_kernel,
        out_shape=(
            jax.ShapeDtypeStruct((ROWS // GROUP, GROUP, D), BF16),
            jax.ShapeDtypeStruct((ROWS, D), BF16),
        ),
        in_specs=[ANY] * 6,
        out_specs=(VMEM, VMEM),
        scratch_shapes=[rows] * 4
        + [
            pltpu.VMEM((D, D), BF16),
            pltpu.VMEM((D, 3 * D), BF16),
            pltpu.VMEM((ROWS, D), BF16),
            pltpu.VMEM((ROWS, 3 * D), BF16),
            pltpu.SemaphoreType.DMA((6,)),
        ],
        cost_estimate=pl.CostEstimate(flops=9 * 10**8, bytes_accessed=4 << 20, transcendentals=300000),
        name="spatial_back",
    )(x, q, k, v, wo, wqkv)


def flatten(refs, flat_ref, first=0):
    for i, ref in enumerate(refs, first):
        flat_ref[i] = ref[...].reshape(ROWS, D)


def attend_kernel(q_ref, k_ref, v_ref, mixed_ref, probs_ref, flat_ref):
    low, same = low_lanes(), same_patch()
    flatten((q_ref, k_ref, v_ref), flat_ref)
    for p in range(PAIRS):
        cols = pl.ds(p * PAIR, PAIR)
        probs = softmax_cols(mm(flat_ref[1, :, cols], stacked(flat_ref[0, :, cols] * BF16(SCALE), low), NT), same)
        probs_ref[p] = probs
        mixed_ref[:, cols] = joined(mm(probs.astype(BF16), flat_ref[2, :, cols], TN), low).astype(BF16)


def attend(q, k, v):
    return pl.pallas_call(
        attend_kernel,
        out_shape=(
            jax.ShapeDtypeStruct((ROWS, D), BF16),
            jax.ShapeDtypeStruct((PAIRS, ROWS, 2 * ROWS), F32),
        ),
        in_specs=[VMEM] * 3,
        out_specs=(VMEM, VMEM),
        scratch_shapes=[pltpu.VMEM((3, ROWS, D), BF16)],
        compiler_params=pltpu.CompilerParams(vmem_limit_bytes=16 << 20),
        cost_estimate=pl.CostEstimate(flops=2 * 10**8, bytes_accessed=2 << 20, transcendentals=300000),
        name="temporal_attend",
    )(q, k, v)


def temporal_kernel(chip_ref, x_hbm, q_hbm, k_hbm, v_hbm, probs_hbm, wo_hbm, wqkv_hbm, keep_ref, send_ref,
                    x_ref, q_ref, k_ref, v_ref, probs_ref, wo_ref, wqkv_ref, dm_ref, dqkv_ref, flat_ref, block_ref, sems):
    pairs = (
        (x_hbm, x_ref), (wo_hbm, wo_ref), (q_hbm, q_ref), (k_hbm, k_ref), (v_hbm, v_ref),
        (probs_hbm, probs_ref), (wqkv_hbm, wqkv_ref),
    )
    copies = [pltpu.make_async_copy(src, dst, sems.at[i]) for i, (src, dst) in enumerate(pairs)]
    for copy in copies:
        copy.start()
    low = low_lanes()
    copies[0].wait()
    flatten((x_ref,), flat_ref)
    x = flat_ref[0]
    copies[1].wait()
    dm_ref[...] = mm(x, wo_ref[...], NT).astype(BF16)
    for copy in copies[2:6]:
        copy.wait()
    flatten((q_ref, k_ref, v_ref), flat_ref, 1)
    for p in range(PAIRS):
        cols = pl.ds(p * PAIR, PAIR)
        q2 = stacked(flat_ref[1, :, cols] * BF16(SCALE), low)
        dm2 = stacked(dm_ref[:, cols], low)
        pair_back(p, probs_ref[p], q2, flat_ref[2, :, cols], flat_ref[3, :, cols], dm2, dqkv_ref, low)
    copies[6].wait()
    out = x.astype(F32) + mm(dqkv_ref[...], wqkv_ref[...], NT)
    block_ref[...] = out.astype(BF16).reshape(ROWS // GROUP, GROUP, D)
    chip = chip_ref[0]
    keep_ref[...] = block_ref[pl.ds(chip * 2 * CHIPS, 2 * CHIPS)]
    send_ref[...] = block_ref[pl.ds((1 - chip) * 2 * CHIPS, 2 * CHIPS)]


def temporal(chip, x, q, k, v, probs, wo, wqkv):
    rows = pltpu.VMEM((ROWS // GROUP, GROUP, D), BF16)
    half = jax.ShapeDtypeStruct((2 * CHIPS, GROUP, D), BF16)
    return pl.pallas_call(
        temporal_kernel,
        out_shape=(half, half),
        in_specs=[pl.BlockSpec(memory_space=pltpu.SMEM)] + [ANY] * 7,
        out_specs=(VMEM, VMEM),
        scratch_shapes=[rows] * 4
        + [
            pltpu.VMEM((PAIRS, ROWS, 2 * ROWS), F32),
            pltpu.VMEM((D, D), BF16),
            pltpu.VMEM((D, 3 * D), BF16),
            pltpu.VMEM((ROWS, D), BF16),
            pltpu.VMEM((ROWS, 3 * D), BF16),
            pltpu.VMEM((4, ROWS, D), BF16),
            rows,
            pltpu.SemaphoreType.DMA((7,)),
        ],
        cost_estimate=pl.CostEstimate(flops=7 * 10**8, bytes_accessed=5 << 20, transcendentals=0),
        name="temporal_back",
    )(chip, x, q, k, v, probs, wo, wqkv)


def outer_kernel(factor, core_ref, mixed_ref, x_ref, send_ref, keep_ref):
    core = core_ref[0]
    x = x_ref[...].reshape(ROWS, D)
    theirs = pl.ds(pl.multiple_of((1 - core) * HALF, HALF), HALF)
    ours = pl.ds(pl.multiple_of(core * HALF, HALF), HALF)
    send_ref[...] = (mm(mixed_ref[:, theirs], x, TN) * factor).astype(BF16)
    keep_ref[...] = mm(mixed_ref[:, ours], x, TN) * factor


def outer(mixed, x, core, factor):
    return pl.pallas_call(
        functools.partial(outer_kernel, factor),
        out_shape=(jax.ShapeDtypeStruct((HALF, D), BF16), jax.ShapeDtypeStruct((HALF, D), F32)),
        in_specs=[pl.BlockSpec(memory_space=pltpu.SMEM), VMEM, VMEM],
        out_specs=(VMEM, VMEM),
        compiler_params=pltpu.CompilerParams(vmem_limit_bytes=16 << 20),
        cost_estimate=pl.CostEstimate(flops=10**8, bytes_accessed=1 << 20, transcendentals=0),
        name="weight_grad",
    )(core, mixed, x)


def fold_kernel(keep_s_ref, got_s_ref, keep_t_ref, got_t_ref, out_ref, sum_ref):
    sum_ref[0:QUARTER, :] = keep_s_ref[...] + got_s_ref[...].astype(F32)
    sum_ref[QUARTER:HALF, :] = keep_t_ref[...] + got_t_ref[...].astype(F32)
    sum_ref[HALF:, :] = jnp.zeros((BANDS * BAND - HALF, D), F32)
    for band in range(BANDS):
        for j in range(PAIRS):
            out_ref[band * PAIRS + j] = sum_ref[
                band * BAND : (band + 1) * BAND, j * LANES : (j + 1) * LANES
            ].astype(BF16)


def fold(keep_s, got_s, keep_t, got_t):
    return pl.pallas_call(
        fold_kernel,
        out_shape=jax.ShapeDtypeStruct((CHIPS, BAND, LANES), BF16),
        in_specs=[VMEM] * 4,
        out_specs=VMEM,
        scratch_shapes=[pltpu.VMEM((BANDS * BAND, D), F32)],
        compiler_params=pltpu.CompilerParams(vmem_limit_bytes=16 << 20),
        cost_estimate=pl.CostEstimate(flops=10**6, bytes_accessed=1 << 20, transcendentals=0),
        name="fold",
    )(keep_s, got_s, keep_t, got_t)


def total_kernel(parts_ref, out_ref):
    total = parts_ref[0].astype(F32)
    for i in range(1, CHIPS):
        total = total + parts_ref[i].astype(F32)
    total = total.astype(BF16)
    for i in range(CHIPS):
        out_ref[i] = total


def total_of(parts):
    return pl.pallas_call(
        total_kernel,
        out_shape=jax.ShapeDtypeStruct((CHIPS, BAND, LANES), BF16),
        in_specs=[VMEM],
        out_specs=VMEM,
        compiler_params=pltpu.CompilerParams(vmem_limit_bytes=16 << 20),
        cost_estimate=pl.CostEstimate(flops=10**6, bytes_accessed=1 << 19, transcendentals=0),
        name="total",
    )(parts)


def place_quarter(source, c, y, outs, buffer, sems):
    for band in range(BANDS):
        for j in range(PAIRS):
            for g in range(2):
                low = max(band * BAND, g * QUARTER)
                high = min((band + 1) * BAND, (g + 1) * QUARTER)
                if low < high:
                    buffer[g, low - g * QUARTER : high - g * QUARTER, j * LANES : (j + 1) * LANES] = source[
                        band * PAIRS + j, low - band * BAND : high - band * BAND, :
                    ].astype(F32)
    rows = pl.ds(pl.multiple_of(c * HALF + y * QUARTER, QUARTER), QUARTER)
    copies = [pltpu.make_async_copy(buffer.at[g], outs[g].at[rows], sems.at[g]) for g in range(2)]
    for copy in copies:
        copy.start()
    return copies


def near_kernel(where_ref, own_ref, beside_ref, first_ref, second_ref, buffers, sems):
    core, chip = where_ref[0], where_ref[1]
    outs = (first_ref, second_ref)
    copies = place_quarter(own_ref, core, chip, outs, buffers.at[0], sems.at[0])
    copies += place_quarter(beside_ref, 1 - core, chip, outs, buffers.at[1], sems.at[1])
    for copy in copies:
        copy.wait()


def far_kernel(where_ref, across_ref, far_ref, blocks_ref, *refs):
    first_ref, second_ref, result_ref, buffers, result, sems, result_sem = refs[2:]
    core, chip = where_ref[0], where_ref[1]
    outs = (first_ref, second_ref)
    copies = place_quarter(across_ref, core, 1 - chip, outs, buffers.at[0], sems.at[0])
    copies += place_quarter(far_ref, 1 - core, 1 - chip, outs, buffers.at[1], sems.at[1])
    for across in range(2):
        rows = pl.ds((chip + across - 2 * chip * across) * CHIPS, CHIPS)
        for c in range(2):
            result[rows, c * GROUP : (c + 1) * GROUP, :] = blocks_ref[:, c, across]
    copies.append(pltpu.make_async_copy(result, result_ref, result_sem))
    copies[-1].start()
    for copy in copies:
        copy.wait()


def place(where, *arrays):
    grad = jax.ShapeDtypeStruct((D, D), F32)
    rows = jax.ShapeDtypeStruct((ROWS // 8, 8, D), BF16)
    final = len(arrays) > 2
    scratch = [pltpu.VMEM((2, 2, QUARTER, D), F32)]
    if final:
        scratch.append(pltpu.VMEM((ROWS // 8, 8, D), BF16))
    scratch.append(pltpu.SemaphoreType.DMA((2, 2)))
    if final:
        scratch.append(pltpu.SemaphoreType.DMA(()))
    return pl.pallas_call(
        far_kernel if final else near_kernel,
        out_shape=(grad, grad, rows) if final else (grad, grad),
        in_specs=[pl.BlockSpec(memory_space=pltpu.SMEM)]
        + ([VMEM] * 3 + [ANY] * 2 if final else [VMEM] * 2),
        out_specs=(ANY,) * (3 if final else 2),
        scratch_shapes=scratch,
        input_output_aliases={4: 0, 5: 1} if final else {},
        compiler_params=pltpu.CompilerParams(vmem_limit_bytes=16 << 20),
        cost_estimate=pl.CostEstimate(flops=10**6, bytes_accessed=3 << 20, transcendentals=0),
        name="place_far" if final else "place_near",
    )(where, *arrays)


def exchanged(blocks):
    return lax.all_to_all(blocks, FRAME, 0, 0, tiled=True)


def on_device(
    cotangent,
    q_spatial,
    k_spatial,
    v_spatial,
    q_temporal,
    k_temporal,
    v_temporal,
    w_qkv_spatial,
    w_out_spatial,
    w_qkv_temporal,
    w_out_temporal,
):
    core = lax.axis_index("frame_2").astype(jnp.int32)
    chip = lax.axis_index("frame_0").astype(jnp.int32)
    core_of = core.reshape(1)
    where = jnp.stack([core, chip])
    factor = 1.0 / math.sqrt(48 * ROWS)

    def over_core(mixed, x):
        send, keep = outer(mixed, x, core_of, factor)
        got = lax.ppermute(send, "frame_2", SWAP)
        both = keep + got.astype(F32)
        theirs = lax.dynamic_slice_in_dim(both, (1 - chip) * QUARTER, QUARTER, 0).astype(BF16)
        ours = lax.dynamic_slice_in_dim(both, chip * QUARTER, QUARTER, 0)
        got = lax.ppermute(theirs, "frame_0", SWAP)
        return ours, got

    d_x1, mixed_s = spatial(cotangent, q_spatial, k_spatial, v_spatial, w_out_spatial, w_qkv_spatial)
    d_x1_t = exchanged(d_x1)
    mixed_t, probs_t = attend(q_temporal, k_temporal, v_temporal)
    keep_s, got_s = over_core(mixed_s, cotangent)
    keep_t, got_t = over_core(mixed_t, d_x1_t)
    pieces = fold(keep_s, got_s, keep_t, got_t)
    parts = lax.all_to_all(pieces, "frame_1", 0, 0, tiled=True)
    near_r, send_r = temporal(
        chip.reshape(1), d_x1_t, q_temporal, k_temporal, v_temporal, probs_t, w_out_temporal, w_qkv_temporal
    )
    far_r = lax.ppermute(send_r, "frame_0", SWAP)
    total = total_of(parts)
    own = lax.all_to_all(total, "frame_1", 0, 0, tiled=True)
    blocks = jnp.stack([near_r, far_r], axis=1)
    blocks = lax.all_to_all(blocks, ("frame_1", "frame_2"), 0, 0, tiled=True)
    blocks = blocks.reshape(CHIPS, 2, 2, GROUP, D)
    across = lax.ppermute(own, "frame_0", SWAP)
    beside = lax.ppermute(own, "frame_2", SWAP)
    far = lax.ppermute(across, "frame_2", SWAP)
    grads = place(where, own, beside)
    first, second, result = place(where, across, far, blocks, *grads)
    return (result.reshape(1, ROWS, D), first, second)


def solution(mesh):
    finer = Mesh(
        mesh.devices.reshape(mesh.shape["clip"], 2, 12, 2),
        ("clip", "frame_0", "frame_1", "frame_2"),
    )
    in_specs = (
        P(CLIP_FRAME, None, None),
        P(CLIP_FRAME, None, None),
        P(CLIP_FRAME, None, None),
        P(CLIP_FRAME, None, None),
        P("clip", FRAME, None),
        P("clip", FRAME, None),
        P("clip", FRAME, None),
        P(),
        P(),
        P(),
        P(),
    )
    out_specs = (P(CLIP_FRAME, None, None), P("clip", None), P("clip", None))
    return jax.shard_map(
        on_device, mesh=finer, in_specs=in_specs, out_specs=out_specs, check_vma=False
    )
```

```python
import functools
import math

import jax
import jax.numpy as jnp
from jax import lax
from jax.experimental import pallas as pl
from jax.experimental.pallas import tpu as pltpu
from jax.sharding import Mesh
from jax.sharding import PartitionSpec as P


D = 512
HEADS = 8
ROWS = 192
GROUP = 4
PAIR = 128
PAIRS = D // PAIR
HALF = D // 2
QUARTER = D // 4
CHIPS = 12
BANDS = 3
BAND = 88
LANES = 128
F32 = jnp.float32
BF16 = jnp.bfloat16
NT = (((1,), (1,)), ((), ()))
TN = (((0,), (0,)), ((), ()))
NN = (((1,), (0,)), ((), ()))
FRAME = ("frame_0", "frame_1", "frame_2")
CLIP_FRAME = ("clip", "frame_0", "frame_1", "frame_2")
SCALE = 1.0 / math.sqrt(D // HEADS)
SWAP = [(0, 1), (1, 0)]
VMEM = pl.BlockSpec(memory_space=pltpu.VMEM)
ANY = pl.BlockSpec(memory_space=pl.ANY)


def mm(a, b, dims):
    return lax.dot_general(a, b, dims, preferred_element_type=F32)


def stacked(x, low):
    zero = jnp.zeros_like(x)
    return jnp.concatenate([jnp.where(low, x, zero), jnp.where(low, zero, x)], axis=0)


def joined(x, low):
    return jnp.where(low, x[:ROWS], x[ROWS:])


def softmax_cols(scores, same):
    if same is not None:
        scores = jnp.where(same, scores, -1e30)
    shifted = jnp.exp(scores - jnp.max(scores, axis=0, keepdims=True))
    return shifted * (1.0 / jnp.sum(shifted, axis=0, keepdims=True))


def low_lanes():
    return lax.broadcasted_iota(jnp.int32, (ROWS, PAIR), 1) < D // HEADS


def same_patch():
    rows = lax.broadcasted_iota(jnp.int32, (ROWS, 2 * ROWS), 0)
    cols = lax.broadcasted_iota(jnp.int32, (ROWS, 2 * ROWS), 1)
    return jnp.bitwise_and(rows - cols, GROUP - 1) == 0


def score_back(probs, v, dm2):
    d_probs = mm(v, dm2, NT)
    inner = jnp.sum(probs * d_probs, axis=0, keepdims=True)
    return (probs * (d_probs - inner)).astype(BF16)


def rows_back(p, probs, d_scores, q2, k, dm2, dqkv_ref, low):
    dqkv_ref[:, pl.ds(p * PAIR, PAIR)] = joined(mm(d_scores, k * BF16(SCALE), TN), low).astype(BF16)
    dqkv_ref[:, pl.ds(D + p * PAIR, PAIR)] = mm(d_scores, q2, NN).astype(BF16)
    dqkv_ref[:, pl.ds(2 * D + p * PAIR, PAIR)] = mm(probs.astype(BF16), dm2, NN).astype(BF16)


def spatial_kernel(x_hbm, q_hbm, k_hbm, v_hbm, wo_hbm, wqkv_hbm, out_ref,
                   x_ref, q_ref, k_ref, v_ref, wo_ref, wqkv_ref, dm_ref, dqkv_ref, probs_ref, d_scores_ref, sems):
    pairs = ((q_hbm, q_ref), (k_hbm, k_ref), (x_hbm, x_ref), (wo_hbm, wo_ref), (v_hbm, v_ref), (wqkv_hbm, wqkv_ref))
    copies = [pltpu.make_async_copy(src, dst, sems.at[i]) for i, (src, dst) in enumerate(pairs)]
    for copy in copies:
        copy.start()
    low = low_lanes()

    def queries(p):
        return stacked(q_ref[0, :, pl.ds(p * PAIR, PAIR)] * BF16(SCALE), low)

    for copy in copies[:2]:
        copy.wait()
    for p in range(PAIRS):
        probs_ref[p] = softmax_cols(mm(k_ref[0, :, pl.ds(p * PAIR, PAIR)], queries(p), NT), None)
    for copy in copies[2:4]:
        copy.wait()
    x = x_ref[0]
    dm_ref[...] = mm(x, wo_ref[...], NT).astype(BF16)
    copies[4].wait()
    for p in range(PAIRS):
        cols = pl.ds(p * PAIR, PAIR)
        d_scores_ref[p] = score_back(probs_ref[p], v_ref[0, :, cols], stacked(dm_ref[:, cols], low))
    for p in range(PAIRS):
        cols = pl.ds(p * PAIR, PAIR)
        dm2 = stacked(dm_ref[:, cols], low)
        rows_back(p, probs_ref[p], d_scores_ref[p], queries(p), k_ref[0, :, cols], dm2, dqkv_ref, low)
    copies[5].wait()
    out = x.astype(F32) + mm(dqkv_ref[...], wqkv_ref[...], NT)
    out_ref[...] = out.astype(BF16).reshape(ROWS // GROUP, GROUP, D)


def spatial(x, q, k, v, wo, wqkv):
    rows = pltpu.VMEM((1, ROWS, D), BF16)
    return pl.pallas_call(
        spatial_kernel,
        out_shape=jax.ShapeDtypeStruct((ROWS // GROUP, GROUP, D), BF16),
        in_specs=[ANY] * 6,
        out_specs=VMEM,
        scratch_shapes=[rows] * 4
        + [
            pltpu.VMEM((D, D), BF16),
            pltpu.VMEM((D, 3 * D), BF16),
            pltpu.VMEM((ROWS, D), BF16),
            pltpu.VMEM((ROWS, 3 * D), BF16),
            pltpu.VMEM((PAIRS, ROWS, 2 * ROWS), F32),
            pltpu.VMEM((PAIRS, ROWS, 2 * ROWS), BF16),
            pltpu.SemaphoreType.DMA((6,)),
        ],
        cost_estimate=pl.CostEstimate(flops=8 * 10**8, bytes_accessed=4 << 20, transcendentals=300000),
        name="spatial_back",
    )(x, q, k, v, wo, wqkv)


def spatial_grad_kernel(factor, core_ref, q_ref, k_ref, v_ref, x_ref, send_ref, keep_ref, mixed_ref):
    low = low_lanes()
    for p in range(PAIRS):
        cols = pl.ds(p * PAIR, PAIR)
        q2 = stacked(q_ref[0, :, cols] * BF16(SCALE), low)
        probs = softmax_cols(mm(k_ref[0, :, cols], q2, NT), None)
        mixed_ref[:, cols] = joined(mm(probs.astype(BF16), v_ref[0, :, cols], TN), low).astype(BF16)
    outer_kernel(factor, core_ref, mixed_ref, x_ref, send_ref, keep_ref)


def spatial_grad(q, k, v, x, core, factor):
    return pl.pallas_call(
        functools.partial(spatial_grad_kernel, factor),
        out_shape=(jax.ShapeDtypeStruct((HALF, D), BF16), jax.ShapeDtypeStruct((HALF, D), F32)),
        in_specs=[pl.BlockSpec(memory_space=pltpu.SMEM)] + [VMEM] * 4,
        out_specs=(VMEM, VMEM),
        scratch_shapes=[pltpu.VMEM((ROWS, D), BF16)],
        compiler_params=pltpu.CompilerParams(vmem_limit_bytes=16 << 20),
        cost_estimate=pl.CostEstimate(flops=3 * 10**8, bytes_accessed=2 << 20, transcendentals=300000),
        name="spatial_grad",
    )(core, q, k, v, x)


def flatten(refs, flat_ref, first=0):
    for i, ref in enumerate(refs, first):
        flat_ref[i] = ref[...].reshape(ROWS, D)


def attend_kernel(q_ref, k_ref, v_ref, mixed_ref, probs_ref, flat_ref):
    low, same = low_lanes(), same_patch()
    flatten((q_ref, k_ref, v_ref), flat_ref)
    for p in range(PAIRS):
        cols = pl.ds(p * PAIR, PAIR)
        probs = softmax_cols(mm(flat_ref[1, :, cols], stacked(flat_ref[0, :, cols] * BF16(SCALE), low), NT), same)
        probs_ref[p] = probs
        mixed_ref[:, cols] = joined(mm(probs.astype(BF16), flat_ref[2, :, cols], TN), low).astype(BF16)


def attend(q, k, v):
    return pl.pallas_call(
        attend_kernel,
        out_shape=(
            jax.ShapeDtypeStruct((ROWS, D), BF16),
            jax.ShapeDtypeStruct((PAIRS, ROWS, 2 * ROWS), F32),
        ),
        in_specs=[VMEM] * 3,
        out_specs=(VMEM, VMEM),
        scratch_shapes=[pltpu.VMEM((3, ROWS, D), BF16)],
        compiler_params=pltpu.CompilerParams(vmem_limit_bytes=16 << 20),
        cost_estimate=pl.CostEstimate(flops=2 * 10**8, bytes_accessed=2 << 20, transcendentals=300000),
        name="temporal_attend",
    )(q, k, v)


def temporal_kernel(chip_ref, x_hbm, q_hbm, k_hbm, v_hbm, probs_hbm, wo_hbm, wqkv_hbm, keep_ref, send_ref,
                    x_ref, q_ref, k_ref, v_ref, probs_ref, wo_ref, wqkv_ref, dm_ref, dqkv_ref, flat_ref, block_ref, d_scores_ref, sems):
    pairs = (
        (x_hbm, x_ref), (wo_hbm, wo_ref), (q_hbm, q_ref), (k_hbm, k_ref), (v_hbm, v_ref),
        (probs_hbm, probs_ref), (wqkv_hbm, wqkv_ref),
    )
    copies = [pltpu.make_async_copy(src, dst, sems.at[i]) for i, (src, dst) in enumerate(pairs)]
    for copy in copies:
        copy.start()
    low = low_lanes()
    copies[0].wait()
    flatten((x_ref,), flat_ref)
    x = flat_ref[0]
    copies[1].wait()
    dm_ref[...] = mm(x, wo_ref[...], NT).astype(BF16)
    for copy in copies[2:6]:
        copy.wait()
    flatten((q_ref, k_ref, v_ref), flat_ref, 1)
    for p in range(PAIRS):
        cols = pl.ds(p * PAIR, PAIR)
        d_scores_ref[p] = score_back(probs_ref[p], flat_ref[3, :, cols], stacked(dm_ref[:, cols], low))
    for p in range(PAIRS):
        cols = pl.ds(p * PAIR, PAIR)
        q2 = stacked(flat_ref[1, :, cols] * BF16(SCALE), low)
        dm2 = stacked(dm_ref[:, cols], low)
        rows_back(p, probs_ref[p], d_scores_ref[p], q2, flat_ref[2, :, cols], dm2, dqkv_ref, low)
    copies[6].wait()
    out = x.astype(F32) + mm(dqkv_ref[...], wqkv_ref[...], NT)
    block_ref[...] = out.astype(BF16).reshape(ROWS // GROUP, GROUP, D)
    chip = chip_ref[0]
    keep_ref[...] = block_ref[pl.ds(chip * 2 * CHIPS, 2 * CHIPS)]
    send_ref[...] = block_ref[pl.ds((1 - chip) * 2 * CHIPS, 2 * CHIPS)]


def temporal(chip, x, q, k, v, probs, wo, wqkv):
    rows = pltpu.VMEM((ROWS // GROUP, GROUP, D), BF16)
    half = jax.ShapeDtypeStruct((2 * CHIPS, GROUP, D), BF16)
    return pl.pallas_call(
        temporal_kernel,
        out_shape=(half, half),
        in_specs=[pl.BlockSpec(memory_space=pltpu.SMEM)] + [ANY] * 7,
        out_specs=(VMEM, VMEM),
        scratch_shapes=[rows] * 4
        + [
            pltpu.VMEM((PAIRS, ROWS, 2 * ROWS), F32),
            pltpu.VMEM((D, D), BF16),
            pltpu.VMEM((D, 3 * D), BF16),
            pltpu.VMEM((ROWS, D), BF16),
            pltpu.VMEM((ROWS, 3 * D), BF16),
            pltpu.VMEM((4, ROWS, D), BF16),
            rows,
            pltpu.VMEM((PAIRS, ROWS, 2 * ROWS), BF16),
            pltpu.SemaphoreType.DMA((7,)),
        ],
        cost_estimate=pl.CostEstimate(flops=7 * 10**8, bytes_accessed=5 << 20, transcendentals=0),
        name="temporal_back",
    )(chip, x, q, k, v, probs, wo, wqkv)


def outer_kernel(factor, core_ref, mixed_ref, x_ref, send_ref, keep_ref):
    core = core_ref[0]
    x = x_ref[...].reshape(ROWS, D)
    theirs = pl.ds(pl.multiple_of((1 - core) * HALF, HALF), HALF)
    ours = pl.ds(pl.multiple_of(core * HALF, HALF), HALF)
    send_ref[...] = (mm(mixed_ref[:, theirs], x, TN) * factor).astype(BF16)
    keep_ref[...] = mm(mixed_ref[:, ours], x, TN) * factor


def outer(mixed, x, core, factor):
    return pl.pallas_call(
        functools.partial(outer_kernel, factor),
        out_shape=(jax.ShapeDtypeStruct((HALF, D), BF16), jax.ShapeDtypeStruct((HALF, D), F32)),
        in_specs=[pl.BlockSpec(memory_space=pltpu.SMEM), VMEM, VMEM],
        out_specs=(VMEM, VMEM),
        compiler_params=pltpu.CompilerParams(vmem_limit_bytes=16 << 20),
        cost_estimate=pl.CostEstimate(flops=10**8, bytes_accessed=1 << 20, transcendentals=0),
        name="weight_grad",
    )(core, mixed, x)


def fold_kernel(keep_s_ref, got_s_ref, keep_t_ref, got_t_ref, out_ref, sum_ref):
    sum_ref[0:QUARTER, :] = keep_s_ref[...] + got_s_ref[...].astype(F32)
    sum_ref[QUARTER:HALF, :] = keep_t_ref[...] + got_t_ref[...].astype(F32)
    sum_ref[HALF:, :] = jnp.zeros((BANDS * BAND - HALF, D), F32)
    for band in range(BANDS):
        for j in range(PAIRS):
            out_ref[band * PAIRS + j] = sum_ref[
                band * BAND : (band + 1) * BAND, j * LANES : (j + 1) * LANES
            ].astype(BF16)


def fold(keep_s, got_s, keep_t, got_t):
    return pl.pallas_call(
        fold_kernel,
        out_shape=jax.ShapeDtypeStruct((CHIPS, BAND, LANES), BF16),
        in_specs=[VMEM] * 4,
        out_specs=VMEM,
        scratch_shapes=[pltpu.VMEM((BANDS * BAND, D), F32)],
        compiler_params=pltpu.CompilerParams(vmem_limit_bytes=16 << 20),
        cost_estimate=pl.CostEstimate(flops=10**6, bytes_accessed=1 << 20, transcendentals=0),
        name="fold",
    )(keep_s, got_s, keep_t, got_t)


def total_kernel(parts_ref, out_ref):
    total = parts_ref[0].astype(F32)
    for i in range(1, CHIPS):
        total = total + parts_ref[i].astype(F32)
    total = total.astype(BF16)
    for i in range(CHIPS):
        out_ref[i] = total


def total_of(parts):
    return pl.pallas_call(
        total_kernel,
        out_shape=jax.ShapeDtypeStruct((CHIPS, BAND, LANES), BF16),
        in_specs=[VMEM],
        out_specs=VMEM,
        compiler_params=pltpu.CompilerParams(vmem_limit_bytes=16 << 20),
        cost_estimate=pl.CostEstimate(flops=10**6, bytes_accessed=1 << 19, transcendentals=0),
        name="total",
    )(parts)


def place_quarter(source, c, y, outs, buffer, sems):
    for band in range(BANDS):
        for j in range(PAIRS):
            for g in range(2):
                low = max(band * BAND, g * QUARTER)
                high = min((band + 1) * BAND, (g + 1) * QUARTER)
                if low < high:
                    buffer[g, low - g * QUARTER : high - g * QUARTER, j * LANES : (j + 1) * LANES] = source[
                        band * PAIRS + j, low - band * BAND : high - band * BAND, :
                    ].astype(F32)
    rows = pl.ds(pl.multiple_of(c * HALF + y * QUARTER, QUARTER), QUARTER)
    copies = [pltpu.make_async_copy(buffer.at[g], outs[g].at[rows], sems.at[g]) for g in range(2)]
    for copy in copies:
        copy.start()
    return copies


def near_kernel(where_ref, own_ref, beside_ref, first_ref, second_ref, buffers, sems):
    core, chip = where_ref[0], where_ref[1]
    outs = (first_ref, second_ref)
    copies = place_quarter(own_ref, core, chip, outs, buffers.at[0], sems.at[0])
    copies += place_quarter(beside_ref, 1 - core, chip, outs, buffers.at[1], sems.at[1])
    for copy in copies:
        copy.wait()


def far_kernel(where_ref, across_ref, far_ref, blocks_ref, *refs):
    first_ref, second_ref, result_ref, buffers, result, sems, result_sem = refs[2:]
    core, chip = where_ref[0], where_ref[1]
    outs = (first_ref, second_ref)
    copies = place_quarter(across_ref, core, 1 - chip, outs, buffers.at[0], sems.at[0])
    copies += place_quarter(far_ref, 1 - core, 1 - chip, outs, buffers.at[1], sems.at[1])
    for across in range(2):
        rows = pl.ds((chip + across - 2 * chip * across) * CHIPS, CHIPS)
        for c in range(2):
            result[rows, c * GROUP : (c + 1) * GROUP, :] = blocks_ref[:, c, across]
    copies.append(pltpu.make_async_copy(result, result_ref, result_sem))
    copies[-1].start()
    for copy in copies:
        copy.wait()


def place(where, *arrays):
    grad = jax.ShapeDtypeStruct((D, D), F32)
    rows = jax.ShapeDtypeStruct((ROWS // 8, 8, D), BF16)
    final = len(arrays) > 2
    scratch = [pltpu.VMEM((2, 2, QUARTER, D), F32)]
    if final:
        scratch.append(pltpu.VMEM((ROWS // 8, 8, D), BF16))
    scratch.append(pltpu.SemaphoreType.DMA((2, 2)))
    if final:
        scratch.append(pltpu.SemaphoreType.DMA(()))
    return pl.pallas_call(
        far_kernel if final else near_kernel,
        out_shape=(grad, grad, rows) if final else (grad, grad),
        in_specs=[pl.BlockSpec(memory_space=pltpu.SMEM)]
        + ([VMEM] * 3 + [ANY] * 2 if final else [VMEM] * 2),
        out_specs=(ANY,) * (3 if final else 2),
        scratch_shapes=scratch,
        input_output_aliases={4: 0, 5: 1} if final else {},
        compiler_params=pltpu.CompilerParams(vmem_limit_bytes=16 << 20),
        cost_estimate=pl.CostEstimate(flops=10**6, bytes_accessed=3 << 20, transcendentals=0),
        name="place_far" if final else "place_near",
    )(where, *arrays)


def exchanged(blocks):
    return lax.all_to_all(blocks, FRAME, 0, 0, tiled=True)


def on_device(
    cotangent,
    q_spatial,
    k_spatial,
    v_spatial,
    q_temporal,
    k_temporal,
    v_temporal,
    w_qkv_spatial,
    w_out_spatial,
    w_qkv_temporal,
    w_out_temporal,
):
    core = lax.axis_index("frame_2").astype(jnp.int32)
    chip = lax.axis_index("frame_0").astype(jnp.int32)
    core_of = core.reshape(1)
    where = jnp.stack([core, chip])
    factor = 1.0 / math.sqrt(48 * ROWS)

    def over_core(send, keep):
        got = lax.ppermute(send, "frame_2", SWAP)
        both = keep + got.astype(F32)
        theirs = lax.dynamic_slice_in_dim(both, (1 - chip) * QUARTER, QUARTER, 0).astype(BF16)
        ours = lax.dynamic_slice_in_dim(both, chip * QUARTER, QUARTER, 0)
        got = lax.ppermute(theirs, "frame_0", SWAP)
        return ours, got

    d_x1 = spatial(cotangent, q_spatial, k_spatial, v_spatial, w_out_spatial, w_qkv_spatial)
    d_x1_t = exchanged(d_x1)
    mixed_t, probs_t = attend(q_temporal, k_temporal, v_temporal)
    halves = spatial_grad(q_spatial, k_spatial, v_spatial, cotangent, core_of, factor)
    keep_s, got_s = over_core(*halves)
    halves = outer(mixed_t, d_x1_t, core_of, factor)
    keep_t, got_t = over_core(*halves)
    pieces = fold(keep_s, got_s, keep_t, got_t)
    parts = lax.all_to_all(pieces, "frame_1", 0, 0, tiled=True)
    near_r, send_r = temporal(
        chip.reshape(1), d_x1_t, q_temporal, k_temporal, v_temporal, probs_t, w_out_temporal, w_qkv_temporal
    )
    far_r = lax.ppermute(send_r, "frame_0", SWAP)
    total = total_of(parts)
    own = lax.all_to_all(total, "frame_1", 0, 0, tiled=True)
    blocks = jnp.stack([near_r, far_r], axis=1)
    blocks = lax.all_to_all(blocks, ("frame_1", "frame_2"), 0, 0, tiled=True)
    blocks = blocks.reshape(CHIPS, 2, 2, GROUP, D)
    across = lax.ppermute(own, "frame_0", SWAP)
    beside = lax.ppermute(own, "frame_2", SWAP)
    far = lax.ppermute(across, "frame_2", SWAP)
    grads = place(where, own, beside)
    first, second, result = place(where, across, far, blocks, *grads)
    return (result.reshape(1, ROWS, D), first, second)


def solution(mesh):
    finer = Mesh(
        mesh.devices.reshape(mesh.shape["clip"], 2, 12, 2),
        ("clip", "frame_0", "frame_1", "frame_2"),
    )
    in_specs = (
        P(CLIP_FRAME, None, None),
        P(CLIP_FRAME, None, None),
        P(CLIP_FRAME, None, None),
        P(CLIP_FRAME, None, None),
        P("clip", FRAME, None),
        P("clip", FRAME, None),
        P("clip", FRAME, None),
        P(),
        P(),
        P(),
        P(),
    )
    out_specs = (P(CLIP_FRAME, None, None), P("clip", None), P("clip", None))
    return jax.shard_map(
        on_device, mesh=finer, in_specs=in_specs, out_specs=out_specs, check_vma=False
    )
```

```python
import functools
import math

import jax
import jax.numpy as jnp
from jax import lax
from jax.experimental import pallas as pl
from jax.experimental.pallas import tpu as pltpu
from jax.sharding import Mesh
from jax.sharding import PartitionSpec as P


D = 512
HEADS = 8
ROWS = 192
GROUP = 4
PAIR = 128
PAIRS = D // PAIR
HALF = D // 2
QUARTER = D // 4
CHIPS = 12
BANDS = 3
BAND = 88
LANES = 128
F32 = jnp.float32
BF16 = jnp.bfloat16
NT = (((1,), (1,)), ((), ()))
TN = (((0,), (0,)), ((), ()))
NN = (((1,), (0,)), ((), ()))
FRAME = ("frame_0", "frame_1", "frame_2")
CLIP_FRAME = ("clip", "frame_0", "frame_1", "frame_2")
SCALE = 1.0 / math.sqrt(D // HEADS)
SWAP = [(0, 1), (1, 0)]
VMEM = pl.BlockSpec(memory_space=pltpu.VMEM)
ANY = pl.BlockSpec(memory_space=pl.ANY)


def mm(a, b, dims):
    return lax.dot_general(a, b, dims, preferred_element_type=F32)


def stacked(x, low):
    zero = jnp.zeros_like(x)
    return jnp.concatenate([jnp.where(low, x, zero), jnp.where(low, zero, x)], axis=0)


def joined(x, low):
    return jnp.where(low, x[:ROWS], x[ROWS:])


def softmax_cols(scores, same):
    if same is not None:
        scores = jnp.where(same, scores, -1e30)
    shifted = jnp.exp(scores - jnp.max(scores, axis=0, keepdims=True))
    return shifted * (1.0 / jnp.sum(shifted, axis=0, keepdims=True))


def low_lanes():
    return lax.broadcasted_iota(jnp.int32, (ROWS, PAIR), 1) < D // HEADS


def same_patch():
    rows = lax.broadcasted_iota(jnp.int32, (ROWS, 2 * ROWS), 0)
    cols = lax.broadcasted_iota(jnp.int32, (ROWS, 2 * ROWS), 1)
    return jnp.bitwise_and(rows - cols, GROUP - 1) == 0


def score_back(probs, v, dm2):
    d_probs = mm(v, dm2, NT)
    inner = jnp.sum(probs * d_probs, axis=0, keepdims=True)
    return (probs * (d_probs - inner)).astype(BF16)


def rows_back(p, probs, d_scores, q2, k, dm2, dqkv_ref, low):
    dqkv_ref[:, pl.ds(p * PAIR, PAIR)] = joined(mm(d_scores, k * BF16(SCALE), TN), low).astype(BF16)
    dqkv_ref[:, pl.ds(D + p * PAIR, PAIR)] = mm(d_scores, q2, NN).astype(BF16)
    dqkv_ref[:, pl.ds(2 * D + p * PAIR, PAIR)] = mm(probs.astype(BF16), dm2, NN).astype(BF16)


def spatial_kernel(x_hbm, q_hbm, k_hbm, v_hbm, wo_hbm, wqkv_hbm, out_ref,
                   x_ref, q_ref, k_ref, v_ref, wo_ref, wqkv_ref, dm_ref, dqkv_ref, probs_ref, d_scores_ref, sems):
    pairs = ((q_hbm, q_ref), (k_hbm, k_ref), (x_hbm, x_ref), (wo_hbm, wo_ref), (v_hbm, v_ref), (wqkv_hbm, wqkv_ref))
    copies = [pltpu.make_async_copy(src, dst, sems.at[i]) for i, (src, dst) in enumerate(pairs)]
    for copy in copies:
        copy.start()
    low = low_lanes()

    def queries(p):
        return stacked(q_ref[0, :, pl.ds(p * PAIR, PAIR)] * BF16(SCALE), low)

    for copy in copies[:2]:
        copy.wait()
    for p in range(PAIRS):
        probs_ref[p] = softmax_cols(mm(k_ref[0, :, pl.ds(p * PAIR, PAIR)], queries(p), NT), None)
    for copy in copies[2:4]:
        copy.wait()
    x = x_ref[0]
    dm_ref[...] = mm(x, wo_ref[...], NT).astype(BF16)
    copies[4].wait()
    for p in range(PAIRS):
        cols = pl.ds(p * PAIR, PAIR)
        d_scores_ref[p] = score_back(probs_ref[p], v_ref[0, :, cols], stacked(dm_ref[:, cols], low))
    for p in range(PAIRS):
        cols = pl.ds(p * PAIR, PAIR)
        dm2 = stacked(dm_ref[:, cols], low)
        rows_back(p, probs_ref[p], d_scores_ref[p], queries(p), k_ref[0, :, cols], dm2, dqkv_ref, low)
    copies[5].wait()
    out = x.astype(F32) + mm(dqkv_ref[...], wqkv_ref[...], NT)
    out_ref[...] = out.astype(BF16).reshape(ROWS // GROUP, GROUP, D)


def spatial(x, q, k, v, wo, wqkv):
    rows = pltpu.VMEM((1, ROWS, D), BF16)
    return pl.pallas_call(
        spatial_kernel,
        out_shape=jax.ShapeDtypeStruct((ROWS // GROUP, GROUP, D), BF16),
        in_specs=[ANY] * 6,
        out_specs=VMEM,
        scratch_shapes=[rows] * 4
        + [
            pltpu.VMEM((D, D), BF16),
            pltpu.VMEM((D, 3 * D), BF16),
            pltpu.VMEM((ROWS, D), BF16),
            pltpu.VMEM((ROWS, 3 * D), BF16),
            pltpu.VMEM((PAIRS, ROWS, 2 * ROWS), F32),
            pltpu.VMEM((PAIRS, ROWS, 2 * ROWS), BF16),
            pltpu.SemaphoreType.DMA((6,)),
        ],
        cost_estimate=pl.CostEstimate(flops=8 * 10**8, bytes_accessed=4 << 20, transcendentals=300000),
        name="spatial_back",
    )(x, q, k, v, wo, wqkv)


def spatial_grad_kernel(factor, core_ref, q_ref, k_ref, v_ref, x_ref, send_ref, keep_ref, mixed_ref):
    low = low_lanes()
    for p in range(PAIRS):
        cols = pl.ds(p * PAIR, PAIR)
        q2 = stacked(q_ref[0, :, cols] * BF16(SCALE), low)
        probs = softmax_cols(mm(k_ref[0, :, cols], q2, NT), None)
        mixed_ref[:, cols] = joined(mm(probs.astype(BF16), v_ref[0, :, cols], TN), low).astype(BF16)
    outer_kernel(factor, core_ref, mixed_ref, x_ref, send_ref, keep_ref)


def spatial_grad(q, k, v, x, core, factor):
    return pl.pallas_call(
        functools.partial(spatial_grad_kernel, factor),
        out_shape=(jax.ShapeDtypeStruct((HALF, D), BF16), jax.ShapeDtypeStruct((HALF, D), F32)),
        in_specs=[pl.BlockSpec(memory_space=pltpu.SMEM)] + [VMEM] * 4,
        out_specs=(VMEM, VMEM),
        scratch_shapes=[pltpu.VMEM((ROWS, D), BF16)],
        compiler_params=pltpu.CompilerParams(vmem_limit_bytes=16 << 20),
        cost_estimate=pl.CostEstimate(flops=3 * 10**8, bytes_accessed=2 << 20, transcendentals=300000),
        name="spatial_grad",
    )(core, q, k, v, x)


def flatten(refs, flat_ref, first=0):
    for i, ref in enumerate(refs, first):
        flat_ref[i] = ref[...].reshape(ROWS, D)


def attend_kernel(q_ref, k_ref, v_ref, mixed_ref, probs_ref, flat_ref):
    low, same = low_lanes(), same_patch()
    flatten((q_ref, k_ref, v_ref), flat_ref)
    for p in range(PAIRS):
        cols = pl.ds(p * PAIR, PAIR)
        probs = softmax_cols(mm(flat_ref[1, :, cols], stacked(flat_ref[0, :, cols] * BF16(SCALE), low), NT), same)
        probs_ref[p] = probs
        mixed_ref[:, cols] = joined(mm(probs.astype(BF16), flat_ref[2, :, cols], TN), low).astype(BF16)


def attend(q, k, v):
    return pl.pallas_call(
        attend_kernel,
        out_shape=(
            jax.ShapeDtypeStruct((ROWS, D), BF16),
            jax.ShapeDtypeStruct((PAIRS, ROWS, 2 * ROWS), F32),
        ),
        in_specs=[VMEM] * 3,
        out_specs=(VMEM, VMEM),
        scratch_shapes=[pltpu.VMEM((3, ROWS, D), BF16)],
        compiler_params=pltpu.CompilerParams(vmem_limit_bytes=16 << 20),
        cost_estimate=pl.CostEstimate(flops=2 * 10**8, bytes_accessed=2 << 20, transcendentals=300000),
        name="temporal_attend",
    )(q, k, v)


def temporal_kernel(chip_ref, x_hbm, q_hbm, k_hbm, v_hbm, probs_hbm, wo_hbm, wqkv_hbm, keep_ref, send_ref,
                    x_ref, q_ref, k_ref, v_ref, probs_ref, wo_ref, wqkv_ref, dm_ref, dqkv_ref, flat_ref, block_ref, d_scores_ref, sems):
    pairs = (
        (x_hbm, x_ref), (wo_hbm, wo_ref), (q_hbm, q_ref), (k_hbm, k_ref), (v_hbm, v_ref),
        (probs_hbm, probs_ref), (wqkv_hbm, wqkv_ref),
    )
    copies = [pltpu.make_async_copy(src, dst, sems.at[i]) for i, (src, dst) in enumerate(pairs)]
    for copy in copies:
        copy.start()
    low = low_lanes()
    copies[0].wait()
    flatten((x_ref,), flat_ref)
    x = flat_ref[0]
    copies[1].wait()
    dm_ref[...] = mm(x, wo_ref[...], NT).astype(BF16)
    for copy in copies[2:6]:
        copy.wait()
    flatten((q_ref, k_ref, v_ref), flat_ref, 1)
    for p in range(PAIRS):
        cols = pl.ds(p * PAIR, PAIR)
        d_scores_ref[p] = score_back(probs_ref[p], flat_ref[3, :, cols], stacked(dm_ref[:, cols], low))
    for p in range(PAIRS):
        cols = pl.ds(p * PAIR, PAIR)
        q2 = stacked(flat_ref[1, :, cols] * BF16(SCALE), low)
        dm2 = stacked(dm_ref[:, cols], low)
        rows_back(p, probs_ref[p], d_scores_ref[p], q2, flat_ref[2, :, cols], dm2, dqkv_ref, low)
    copies[6].wait()
    out = x.astype(F32) + mm(dqkv_ref[...], wqkv_ref[...], NT)
    block_ref[...] = out.astype(BF16).reshape(ROWS // GROUP, GROUP, D)
    chip = chip_ref[0]
    keep_ref[...] = block_ref[pl.ds(chip * 2 * CHIPS, 2 * CHIPS)]
    send_ref[...] = block_ref[pl.ds((1 - chip) * 2 * CHIPS, 2 * CHIPS)]


def temporal(chip, x, q, k, v, probs, wo, wqkv):
    rows = pltpu.VMEM((ROWS // GROUP, GROUP, D), BF16)
    half = jax.ShapeDtypeStruct((2 * CHIPS, GROUP, D), BF16)
    return pl.pallas_call(
        temporal_kernel,
        out_shape=(half, half),
        in_specs=[pl.BlockSpec(memory_space=pltpu.SMEM)] + [ANY] * 7,
        out_specs=(VMEM, VMEM),
        scratch_shapes=[rows] * 4
        + [
            pltpu.VMEM((PAIRS, ROWS, 2 * ROWS), F32),
            pltpu.VMEM((D, D), BF16),
            pltpu.VMEM((D, 3 * D), BF16),
            pltpu.VMEM((ROWS, D), BF16),
            pltpu.VMEM((ROWS, 3 * D), BF16),
            pltpu.VMEM((4, ROWS, D), BF16),
            rows,
            pltpu.VMEM((PAIRS, ROWS, 2 * ROWS), BF16),
            pltpu.SemaphoreType.DMA((7,)),
        ],
        cost_estimate=pl.CostEstimate(flops=7 * 10**8, bytes_accessed=5 << 20, transcendentals=0),
        name="temporal_back",
    )(chip, x, q, k, v, probs, wo, wqkv)


def order_kernel(core_ref, near_ref, far_ref, keep_ref, send_ref):
    core = core_ref[0]
    for i, source in enumerate((near_ref, far_ref)):
        keep_ref[:, i : i + 1] = source[:, pl.ds(core, 1)]
        send_ref[:, i : i + 1] = source[:, pl.ds(1 - core, 1)]


def order(core, near, far):
    half = jax.ShapeDtypeStruct((CHIPS, 2, GROUP, D), BF16)
    return pl.pallas_call(
        order_kernel,
        out_shape=(half, half),
        in_specs=[pl.BlockSpec(memory_space=pltpu.SMEM), VMEM, VMEM],
        out_specs=(VMEM, VMEM),
        compiler_params=pltpu.CompilerParams(vmem_limit_bytes=16 << 20),
        cost_estimate=pl.CostEstimate(flops=10**5, bytes_accessed=1 << 19, transcendentals=0),
        name="order",
    )(core, near.reshape(half.shape), far.reshape(half.shape))


def outer_kernel(factor, core_ref, mixed_ref, x_ref, send_ref, keep_ref):
    core = core_ref[0]
    x = x_ref[...].reshape(ROWS, D)
    theirs = pl.ds(pl.multiple_of((1 - core) * HALF, HALF), HALF)
    ours = pl.ds(pl.multiple_of(core * HALF, HALF), HALF)
    send_ref[...] = (mm(mixed_ref[:, theirs], x, TN) * factor).astype(BF16)
    keep_ref[...] = mm(mixed_ref[:, ours], x, TN) * factor


def outer(mixed, x, core, factor):
    return pl.pallas_call(
        functools.partial(outer_kernel, factor),
        out_shape=(jax.ShapeDtypeStruct((HALF, D), BF16), jax.ShapeDtypeStruct((HALF, D), F32)),
        in_specs=[pl.BlockSpec(memory_space=pltpu.SMEM), VMEM, VMEM],
        out_specs=(VMEM, VMEM),
        compiler_params=pltpu.CompilerParams(vmem_limit_bytes=16 << 20),
        cost_estimate=pl.CostEstimate(flops=10**8, bytes_accessed=1 << 20, transcendentals=0),
        name="weight_grad",
    )(core, mixed, x)


def fold_kernel(keep_s_ref, got_s_ref, keep_t_ref, got_t_ref, out_ref, sum_ref):
    sum_ref[0:QUARTER, :] = keep_s_ref[...] + got_s_ref[...].astype(F32)
    sum_ref[QUARTER:HALF, :] = keep_t_ref[...] + got_t_ref[...].astype(F32)
    sum_ref[HALF:, :] = jnp.zeros((BANDS * BAND - HALF, D), F32)
    for band in range(BANDS):
        for j in range(PAIRS):
            out_ref[band * PAIRS + j] = sum_ref[
                band * BAND : (band + 1) * BAND, j * LANES : (j + 1) * LANES
            ].astype(BF16)


def fold(keep_s, got_s, keep_t, got_t):
    return pl.pallas_call(
        fold_kernel,
        out_shape=jax.ShapeDtypeStruct((CHIPS, BAND, LANES), BF16),
        in_specs=[VMEM] * 4,
        out_specs=VMEM,
        scratch_shapes=[pltpu.VMEM((BANDS * BAND, D), F32)],
        compiler_params=pltpu.CompilerParams(vmem_limit_bytes=16 << 20),
        cost_estimate=pl.CostEstimate(flops=10**6, bytes_accessed=1 << 20, transcendentals=0),
        name="fold",
    )(keep_s, got_s, keep_t, got_t)


def total_kernel(parts_ref, out_ref):
    total = parts_ref[0].astype(F32)
    for i in range(1, CHIPS):
        total = total + parts_ref[i].astype(F32)
    total = total.astype(BF16)
    for i in range(CHIPS):
        out_ref[i] = total


def total_of(parts):
    return pl.pallas_call(
        total_kernel,
        out_shape=jax.ShapeDtypeStruct((CHIPS, BAND, LANES), BF16),
        in_specs=[VMEM],
        out_specs=VMEM,
        compiler_params=pltpu.CompilerParams(vmem_limit_bytes=16 << 20),
        cost_estimate=pl.CostEstimate(flops=10**6, bytes_accessed=1 << 19, transcendentals=0),
        name="total",
    )(parts)


def place_quarter(source, c, y, outs, buffer, sems):
    for band in range(BANDS):
        for j in range(PAIRS):
            for g in range(2):
                low = max(band * BAND, g * QUARTER)
                high = min((band + 1) * BAND, (g + 1) * QUARTER)
                if low < high:
                    buffer[g, low - g * QUARTER : high - g * QUARTER, j * LANES : (j + 1) * LANES] = source[
                        band * PAIRS + j, low - band * BAND : high - band * BAND, :
                    ].astype(F32)
    rows = pl.ds(pl.multiple_of(c * HALF + y * QUARTER, QUARTER), QUARTER)
    copies = [pltpu.make_async_copy(buffer.at[g], outs[g].at[rows], sems.at[g]) for g in range(2)]
    for copy in copies:
        copy.start()
    return copies


def near_kernel(where_ref, own_ref, beside_ref, first_ref, second_ref, buffers, sems):
    core, chip = where_ref[0], where_ref[1]
    outs = (first_ref, second_ref)
    copies = place_quarter(own_ref, core, chip, outs, buffers.at[0], sems.at[0])
    copies += place_quarter(beside_ref, 1 - core, chip, outs, buffers.at[1], sems.at[1])
    for copy in copies:
        copy.wait()


def far_kernel(where_ref, across_ref, far_ref, blocks_ref, *refs):
    first_ref, second_ref, result_ref, buffers, result, sems, result_sem = refs[2:]
    core, chip = where_ref[0], where_ref[1]
    outs = (first_ref, second_ref)
    copies = place_quarter(across_ref, core, 1 - chip, outs, buffers.at[0], sems.at[0])
    copies += place_quarter(far_ref, 1 - core, 1 - chip, outs, buffers.at[1], sems.at[1])
    for across in range(2):
        rows = pl.ds((chip + across - 2 * chip * across) * CHIPS, CHIPS)
        near = blocks_ref[:, across].astype(F32)
        beside = blocks_ref[:, 2 + across].astype(F32)
        result[rows, 0:GROUP, :] = jnp.where(core == 0, near, beside).astype(BF16)
        result[rows, GROUP : 2 * GROUP, :] = jnp.where(core == 0, beside, near).astype(BF16)
    copies.append(pltpu.make_async_copy(result, result_ref, result_sem))
    copies[-1].start()
    for copy in copies:
        copy.wait()


def place(where, *arrays):
    grad = jax.ShapeDtypeStruct((D, D), F32)
    rows = jax.ShapeDtypeStruct((ROWS // 8, 8, D), BF16)
    final = len(arrays) > 2
    scratch = [pltpu.VMEM((2, 2, QUARTER, D), F32)]
    if final:
        scratch.append(pltpu.VMEM((ROWS // 8, 8, D), BF16))
    scratch.append(pltpu.SemaphoreType.DMA((2, 2)))
    if final:
        scratch.append(pltpu.SemaphoreType.DMA(()))
    return pl.pallas_call(
        far_kernel if final else near_kernel,
        out_shape=(grad, grad, rows) if final else (grad, grad),
        in_specs=[pl.BlockSpec(memory_space=pltpu.SMEM)]
        + ([VMEM] * 3 + [ANY] * 2 if final else [VMEM] * 2),
        out_specs=(ANY,) * (3 if final else 2),
        scratch_shapes=scratch,
        input_output_aliases={4: 0, 5: 1} if final else {},
        compiler_params=pltpu.CompilerParams(vmem_limit_bytes=16 << 20),
        cost_estimate=pl.CostEstimate(flops=10**6, bytes_accessed=3 << 20, transcendentals=0),
        name="place_far" if final else "place_near",
    )(where, *arrays)


def exchanged(blocks):
    return lax.all_to_all(blocks, FRAME, 0, 0, tiled=True)


def on_device(
    cotangent,
    q_spatial,
    k_spatial,
    v_spatial,
    q_temporal,
    k_temporal,
    v_temporal,
    w_qkv_spatial,
    w_out_spatial,
    w_qkv_temporal,
    w_out_temporal,
):
    core = lax.axis_index("frame_2").astype(jnp.int32)
    chip = lax.axis_index("frame_0").astype(jnp.int32)
    core_of = core.reshape(1)
    where = jnp.stack([core, chip])
    factor = 1.0 / math.sqrt(48 * ROWS)

    def over_core(send, keep):
        got = lax.ppermute(send, "frame_2", SWAP)
        both = keep + got.astype(F32)
        theirs = lax.dynamic_slice_in_dim(both, (1 - chip) * QUARTER, QUARTER, 0).astype(BF16)
        ours = lax.dynamic_slice_in_dim(both, chip * QUARTER, QUARTER, 0)
        got = lax.ppermute(theirs, "frame_0", SWAP)
        return ours, got

    d_x1 = spatial(cotangent, q_spatial, k_spatial, v_spatial, w_out_spatial, w_qkv_spatial)
    d_x1_t = exchanged(d_x1)
    mixed_t, probs_t = attend(q_temporal, k_temporal, v_temporal)
    halves = spatial_grad(q_spatial, k_spatial, v_spatial, cotangent, core_of, factor)
    keep_s, got_s = over_core(*halves)
    halves = outer(mixed_t, d_x1_t, core_of, factor)
    keep_t, got_t = over_core(*halves)
    pieces = fold(keep_s, got_s, keep_t, got_t)
    parts = lax.all_to_all(pieces, "frame_1", 0, 0, tiled=True)
    near_r, send_r = temporal(
        chip.reshape(1), d_x1_t, q_temporal, k_temporal, v_temporal, probs_t, w_out_temporal, w_qkv_temporal
    )
    far_r = lax.ppermute(send_r, "frame_0", SWAP)
    total = total_of(parts)
    own = lax.all_to_all(total, "frame_1", 0, 0, tiled=True)
    keep_r, send_r = order(core_of, near_r, far_r)
    got_r = lax.ppermute(send_r, "frame_2", SWAP)
    blocks = jnp.concatenate([keep_r, got_r], axis=1)
    blocks = lax.all_to_all(blocks, "frame_1", 0, 0, tiled=True)
    across = lax.ppermute(own, "frame_0", SWAP)
    beside = lax.ppermute(own, "frame_2", SWAP)
    far = lax.ppermute(across, "frame_2", SWAP)
    grads = place(where, own, beside)
    first, second, result = place(where, across, far, blocks, *grads)
    return (result.reshape(1, ROWS, D), first, second)


def solution(mesh):
    finer = Mesh(
        mesh.devices.reshape(mesh.shape["clip"], 2, 12, 2),
        ("clip", "frame_0", "frame_1", "frame_2"),
    )
    in_specs = (
        P(CLIP_FRAME, None, None),
        P(CLIP_FRAME, None, None),
        P(CLIP_FRAME, None, None),
        P(CLIP_FRAME, None, None),
        P("clip", FRAME, None),
        P("clip", FRAME, None),
        P("clip", FRAME, None),
        P(),
        P(),
        P(),
        P(),
    )
    out_specs = (P(CLIP_FRAME, None, None), P("clip", None), P("clip", None))
    return jax.shard_map(
        on_device, mesh=finer, in_specs=in_specs, out_specs=out_specs, check_vma=False
    )
```

```python
import functools
import math

import jax
import jax.numpy as jnp
from jax import lax
from jax.experimental import pallas as pl
from jax.experimental.pallas import tpu as pltpu
from jax.sharding import Mesh
from jax.sharding import PartitionSpec as P


D = 512
HEADS = 8
ROWS = 192
GROUP = 4
PAIR = 128
PAIRS = D // PAIR
HALF = D // 2
QUARTER = D // 4
CHIPS = 12
BANDS = 3
BAND = 88
LANES = 128
F32 = jnp.float32
BF16 = jnp.bfloat16
NT = (((1,), (1,)), ((), ()))
TN = (((0,), (0,)), ((), ()))
NN = (((1,), (0,)), ((), ()))
FRAME = ("frame_0", "frame_1", "frame_2")
CLIP_FRAME = ("clip", "frame_0", "frame_1", "frame_2")
SCALE = 1.0 / math.sqrt(D // HEADS)
SWAP = [(0, 1), (1, 0)]
VMEM = pl.BlockSpec(memory_space=pltpu.VMEM)
ANY = pl.BlockSpec(memory_space=pl.ANY)


def mm(a, b, dims):
    return lax.dot_general(a, b, dims, preferred_element_type=F32)


def stacked(x, low):
    zero = jnp.zeros_like(x)
    return jnp.concatenate([jnp.where(low, x, zero), jnp.where(low, zero, x)], axis=0)


def joined(x, low):
    return jnp.where(low, x[:ROWS], x[ROWS:])


def softmax_cols(scores, same):
    if same is not None:
        scores = jnp.where(same, scores, -1e30)
    shifted = jnp.exp(scores - jnp.max(scores, axis=0, keepdims=True))
    return shifted * (1.0 / jnp.sum(shifted, axis=0, keepdims=True))


def low_lanes():
    return lax.broadcasted_iota(jnp.int32, (ROWS, PAIR), 1) < D // HEADS


def same_patch():
    rows = lax.broadcasted_iota(jnp.int32, (ROWS, 2 * ROWS), 0)
    cols = lax.broadcasted_iota(jnp.int32, (ROWS, 2 * ROWS), 1)
    return jnp.bitwise_and(rows - cols, GROUP - 1) == 0


def score_back(probs, v, dm2):
    d_probs = mm(v, dm2, NT)
    inner = jnp.sum(probs * d_probs, axis=0, keepdims=True)
    return (probs * (d_probs - inner)).astype(BF16)


def rows_back(p, probs, d_scores, q2, k, dm2, dqkv_ref, low):
    dqkv_ref[:, pl.ds(p * PAIR, PAIR)] = joined(mm(d_scores, k * BF16(SCALE), TN), low).astype(BF16)
    dqkv_ref[:, pl.ds(D + p * PAIR, PAIR)] = mm(d_scores, q2, NN).astype(BF16)
    dqkv_ref[:, pl.ds(2 * D + p * PAIR, PAIR)] = mm(probs.astype(BF16), dm2, NN).astype(BF16)


def spatial_kernel(x_hbm, q_hbm, k_hbm, v_hbm, wo_hbm, wqkv_hbm, out_ref,
                   x_ref, q_ref, k_ref, v_ref, wo_ref, wqkv_ref, dm_ref, dqkv_ref, probs_ref, d_scores_ref, sems):
    pairs = ((q_hbm, q_ref), (k_hbm, k_ref), (x_hbm, x_ref), (wo_hbm, wo_ref), (v_hbm, v_ref), (wqkv_hbm, wqkv_ref))
    copies = [pltpu.make_async_copy(src, dst, sems.at[i]) for i, (src, dst) in enumerate(pairs)]
    for copy in copies:
        copy.start()
    low = low_lanes()

    def queries(p):
        return stacked(q_ref[0, :, pl.ds(p * PAIR, PAIR)] * BF16(SCALE), low)

    for copy in copies[:2]:
        copy.wait()
    for p in range(PAIRS):
        probs_ref[p] = softmax_cols(mm(k_ref[0, :, pl.ds(p * PAIR, PAIR)], queries(p), NT), None)
    for copy in copies[2:4]:
        copy.wait()
    x = x_ref[0]
    dm_ref[...] = mm(x, wo_ref[...], NT).astype(BF16)
    copies[4].wait()
    for p in range(PAIRS):
        cols = pl.ds(p * PAIR, PAIR)
        d_scores_ref[p] = score_back(probs_ref[p], v_ref[0, :, cols], stacked(dm_ref[:, cols], low))
    for p in range(PAIRS):
        cols = pl.ds(p * PAIR, PAIR)
        dm2 = stacked(dm_ref[:, cols], low)
        rows_back(p, probs_ref[p], d_scores_ref[p], queries(p), k_ref[0, :, cols], dm2, dqkv_ref, low)
    copies[5].wait()
    out = x.astype(F32) + mm(dqkv_ref[...], wqkv_ref[...], NT)
    out_ref[...] = out.astype(BF16).reshape(ROWS // GROUP, GROUP, D)


def spatial(x, q, k, v, wo, wqkv):
    rows = pltpu.VMEM((1, ROWS, D), BF16)
    return pl.pallas_call(
        spatial_kernel,
        out_shape=jax.ShapeDtypeStruct((ROWS // GROUP, GROUP, D), BF16),
        in_specs=[ANY] * 6,
        out_specs=VMEM,
        scratch_shapes=[rows] * 4
        + [
            pltpu.VMEM((D, D), BF16),
            pltpu.VMEM((D, 3 * D), BF16),
            pltpu.VMEM((ROWS, D), BF16),
            pltpu.VMEM((ROWS, 3 * D), BF16),
            pltpu.VMEM((PAIRS, ROWS, 2 * ROWS), F32),
            pltpu.VMEM((PAIRS, ROWS, 2 * ROWS), BF16),
            pltpu.SemaphoreType.DMA((6,)),
        ],
        cost_estimate=pl.CostEstimate(flops=8 * 10**8, bytes_accessed=4 << 20, transcendentals=300000),
        name="spatial_back",
    )(x, q, k, v, wo, wqkv)


def spatial_grad_kernel(factor, core_ref, q_ref, k_ref, v_ref, x_ref, send_ref, keep_ref, mixed_ref):
    low = low_lanes()
    for p in range(PAIRS):
        cols = pl.ds(p * PAIR, PAIR)
        q2 = stacked(q_ref[0, :, cols] * BF16(SCALE), low)
        probs = softmax_cols(mm(k_ref[0, :, cols], q2, NT), None)
        mixed_ref[:, cols] = joined(mm(probs.astype(BF16), v_ref[0, :, cols], TN), low).astype(BF16)
    outer_kernel(factor, core_ref, mixed_ref, x_ref, send_ref, keep_ref)


def spatial_grad(q, k, v, x, core, factor):
    return pl.pallas_call(
        functools.partial(spatial_grad_kernel, factor),
        out_shape=(jax.ShapeDtypeStruct((HALF, D), BF16), jax.ShapeDtypeStruct((HALF, D), F32)),
        in_specs=[pl.BlockSpec(memory_space=pltpu.SMEM)] + [VMEM] * 4,
        out_specs=(VMEM, VMEM),
        scratch_shapes=[pltpu.VMEM((ROWS, D), BF16)],
        compiler_params=pltpu.CompilerParams(vmem_limit_bytes=16 << 20),
        cost_estimate=pl.CostEstimate(flops=3 * 10**8, bytes_accessed=2 << 20, transcendentals=300000),
        name="spatial_grad",
    )(core, q, k, v, x)


def flatten(refs, flat_ref, first=0):
    for i, ref in enumerate(refs, first):
        flat_ref[i] = ref[...].reshape(ROWS, D)


def attend_kernel(q_ref, k_ref, v_ref, mixed_ref, probs_ref, flat_ref):
    low, same = low_lanes(), same_patch()
    flatten((q_ref, k_ref, v_ref), flat_ref)
    for p in range(PAIRS):
        cols = pl.ds(p * PAIR, PAIR)
        probs = softmax_cols(mm(flat_ref[1, :, cols], stacked(flat_ref[0, :, cols] * BF16(SCALE), low), NT), same)
        probs_ref[p] = probs
        mixed_ref[:, cols] = joined(mm(probs.astype(BF16), flat_ref[2, :, cols], TN), low).astype(BF16)


def attend(q, k, v):
    return pl.pallas_call(
        attend_kernel,
        out_shape=(
            jax.ShapeDtypeStruct((ROWS, D), BF16),
            jax.ShapeDtypeStruct((PAIRS, ROWS, 2 * ROWS), F32),
        ),
        in_specs=[VMEM] * 3,
        out_specs=(VMEM, VMEM),
        scratch_shapes=[pltpu.VMEM((3, ROWS, D), BF16)],
        compiler_params=pltpu.CompilerParams(vmem_limit_bytes=16 << 20),
        cost_estimate=pl.CostEstimate(flops=2 * 10**8, bytes_accessed=2 << 20, transcendentals=300000),
        name="temporal_attend",
    )(q, k, v)


def temporal_kernel(chip_ref, x_hbm, q_hbm, k_hbm, v_hbm, probs_hbm, wo_hbm, wqkv_hbm, keep_ref, send_ref,
                    x_ref, q_ref, k_ref, v_ref, probs_ref, wo_ref, wqkv_ref, dm_ref, dqkv_ref, flat_ref, block_ref, d_scores_ref, sems):
    pairs = (
        (x_hbm, x_ref), (wo_hbm, wo_ref), (q_hbm, q_ref), (k_hbm, k_ref), (v_hbm, v_ref),
        (probs_hbm, probs_ref), (wqkv_hbm, wqkv_ref),
    )
    copies = [pltpu.make_async_copy(src, dst, sems.at[i]) for i, (src, dst) in enumerate(pairs)]
    for copy in copies:
        copy.start()
    low = low_lanes()
    copies[0].wait()
    flatten((x_ref,), flat_ref)
    x = flat_ref[0]
    copies[1].wait()
    dm_ref[...] = mm(x, wo_ref[...], NT).astype(BF16)
    for copy in copies[2:6]:
        copy.wait()
    flatten((q_ref, k_ref, v_ref), flat_ref, 1)
    for p in range(PAIRS):
        cols = pl.ds(p * PAIR, PAIR)
        d_scores_ref[p] = score_back(probs_ref[p], flat_ref[3, :, cols], stacked(dm_ref[:, cols], low))
    for p in range(PAIRS):
        cols = pl.ds(p * PAIR, PAIR)
        q2 = stacked(flat_ref[1, :, cols] * BF16(SCALE), low)
        dm2 = stacked(dm_ref[:, cols], low)
        rows_back(p, probs_ref[p], d_scores_ref[p], q2, flat_ref[2, :, cols], dm2, dqkv_ref, low)
    copies[6].wait()
    out = x.astype(F32) + mm(dqkv_ref[...], wqkv_ref[...], NT)
    block_ref[...] = out.astype(BF16).reshape(ROWS // GROUP, GROUP, D)
    chip = chip_ref[0]
    keep_ref[...] = block_ref[pl.ds(chip * 2 * CHIPS, 2 * CHIPS)]
    send_ref[...] = block_ref[pl.ds((1 - chip) * 2 * CHIPS, 2 * CHIPS)]


def temporal(chip, x, q, k, v, probs, wo, wqkv):
    rows = pltpu.VMEM((ROWS // GROUP, GROUP, D), BF16)
    half = jax.ShapeDtypeStruct((2 * CHIPS, GROUP, D), BF16)
    return pl.pallas_call(
        temporal_kernel,
        out_shape=(half, half),
        in_specs=[pl.BlockSpec(memory_space=pltpu.SMEM)] + [ANY] * 7,
        out_specs=(VMEM, VMEM),
        scratch_shapes=[rows] * 4
        + [
            pltpu.VMEM((PAIRS, ROWS, 2 * ROWS), F32),
            pltpu.VMEM((D, D), BF16),
            pltpu.VMEM((D, 3 * D), BF16),
            pltpu.VMEM((ROWS, D), BF16),
            pltpu.VMEM((ROWS, 3 * D), BF16),
            pltpu.VMEM((4, ROWS, D), BF16),
            rows,
            pltpu.VMEM((PAIRS, ROWS, 2 * ROWS), BF16),
            pltpu.SemaphoreType.DMA((7,)),
        ],
        cost_estimate=pl.CostEstimate(flops=7 * 10**8, bytes_accessed=5 << 20, transcendentals=0),
        name="temporal_back",
    )(chip, x, q, k, v, probs, wo, wqkv)


def order_kernel(core_ref, near_ref, far_ref, keep_ref, send_ref):
    core = core_ref[0]
    for i, source in enumerate((near_ref, far_ref)):
        keep_ref[:, i : i + 1] = source[:, pl.ds(core, 1)]
        send_ref[:, i : i + 1] = source[:, pl.ds(1 - core, 1)]


def order(core, near, far):
    half = jax.ShapeDtypeStruct((CHIPS, 2, GROUP, D), BF16)
    return pl.pallas_call(
        order_kernel,
        out_shape=(half, half),
        in_specs=[pl.BlockSpec(memory_space=pltpu.SMEM), VMEM, VMEM],
        out_specs=(VMEM, VMEM),
        compiler_params=pltpu.CompilerParams(vmem_limit_bytes=16 << 20),
        cost_estimate=pl.CostEstimate(flops=10**5, bytes_accessed=1 << 19, transcendentals=0),
        name="order",
    )(core, near.reshape(half.shape), far.reshape(half.shape))


def outer_kernel(factor, core_ref, mixed_ref, x_ref, send_ref, keep_ref):
    core = core_ref[0]
    x = x_ref[...].reshape(ROWS, D)
    theirs = pl.ds(pl.multiple_of((1 - core) * HALF, HALF), HALF)
    ours = pl.ds(pl.multiple_of(core * HALF, HALF), HALF)
    send_ref[...] = (mm(mixed_ref[:, theirs], x, TN) * factor).astype(BF16)
    keep_ref[...] = mm(mixed_ref[:, ours], x, TN) * factor


def fold_kernel(keep_s_ref, got_s_ref, parts_t_ref, out_ref, sum_ref):
    sum_ref[0:QUARTER, :] = keep_s_ref[...] + got_s_ref[...].astype(F32)
    parts = [parts_t_ref[i].astype(F32) for i in range(4)]
    sum_ref[QUARTER:HALF, :] = (parts[0] + parts[1]) + (parts[2] + parts[3])
    sum_ref[HALF:, :] = jnp.zeros((BANDS * BAND - HALF, D), F32)
    for band in range(BANDS):
        for j in range(PAIRS):
            out_ref[band * PAIRS + j] = sum_ref[
                band * BAND : (band + 1) * BAND, j * LANES : (j + 1) * LANES
            ].astype(BF16)


def fold(keep_s, got_s, parts_t):
    return pl.pallas_call(
        fold_kernel,
        out_shape=jax.ShapeDtypeStruct((CHIPS, BAND, LANES), BF16),
        in_specs=[VMEM] * 3,
        out_specs=VMEM,
        scratch_shapes=[pltpu.VMEM((BANDS * BAND, D), F32)],
        compiler_params=pltpu.CompilerParams(vmem_limit_bytes=16 << 20),
        cost_estimate=pl.CostEstimate(flops=10**6, bytes_accessed=1 << 20, transcendentals=0),
        name="fold",
    )(keep_s, got_s, parts_t)


def total_kernel(parts_ref, out_ref):
    total = parts_ref[0].astype(F32)
    for i in range(1, CHIPS):
        total = total + parts_ref[i].astype(F32)
    total = total.astype(BF16)
    for i in range(CHIPS):
        out_ref[i] = total


def total_of(parts):
    return pl.pallas_call(
        total_kernel,
        out_shape=jax.ShapeDtypeStruct((CHIPS, BAND, LANES), BF16),
        in_specs=[VMEM],
        out_specs=VMEM,
        compiler_params=pltpu.CompilerParams(vmem_limit_bytes=16 << 20),
        cost_estimate=pl.CostEstimate(flops=10**6, bytes_accessed=1 << 19, transcendentals=0),
        name="total",
    )(parts)


def quarters_kernel(factor, mixed_ref, x_ref, out_ref):
    x = x_ref[...].reshape(ROWS, D)
    for y in range(2):
        for c in range(2):
            cols = pl.ds(c * HALF + y * QUARTER, QUARTER)
            out_ref[2 * y + c] = (mm(mixed_ref[:, cols], x, TN) * factor).astype(BF16)


def quarters(mixed, x, factor):
    return pl.pallas_call(
        functools.partial(quarters_kernel, factor),
        out_shape=jax.ShapeDtypeStruct((4, QUARTER, D), BF16),
        in_specs=[VMEM, VMEM],
        out_specs=VMEM,
        compiler_params=pltpu.CompilerParams(vmem_limit_bytes=16 << 20),
        cost_estimate=pl.CostEstimate(flops=10**8, bytes_accessed=1 << 20, transcendentals=0),
        name="weight_grad",
    )(mixed, x)


def place_quarter(source, c, y, outs, buffer, sems):
    for band in range(BANDS):
        for j in range(PAIRS):
            for g in range(2):
                low = max(band * BAND, g * QUARTER)
                high = min((band + 1) * BAND, (g + 1) * QUARTER)
                if low < high:
                    buffer[g, low - g * QUARTER : high - g * QUARTER, j * LANES : (j + 1) * LANES] = source[
                        band * PAIRS + j, low - band * BAND : high - band * BAND, :
                    ].astype(F32)
    rows = pl.ds(pl.multiple_of(c * HALF + y * QUARTER, QUARTER), QUARTER)
    copies = [pltpu.make_async_copy(buffer.at[g], outs[g].at[rows], sems.at[g]) for g in range(2)]
    for copy in copies:
        copy.start()
    return copies


def near_kernel(where_ref, own_ref, beside_ref, first_ref, second_ref, buffers, sems):
    core, chip = where_ref[0], where_ref[1]
    outs = (first_ref, second_ref)
    copies = place_quarter(own_ref, core, chip, outs, buffers.at[0], sems.at[0])
    copies += place_quarter(beside_ref, 1 - core, chip, outs, buffers.at[1], sems.at[1])
    for copy in copies:
        copy.wait()


def far_kernel(where_ref, across_ref, far_ref, blocks_ref, *refs):
    first_ref, second_ref, result_ref, buffers, result, sems, result_sem = refs[2:]
    core, chip = where_ref[0], where_ref[1]
    outs = (first_ref, second_ref)
    copies = place_quarter(across_ref, core, 1 - chip, outs, buffers.at[0], sems.at[0])
    copies += place_quarter(far_ref, 1 - core, 1 - chip, outs, buffers.at[1], sems.at[1])
    for across in range(2):
        rows = pl.ds((chip + across - 2 * chip * across) * CHIPS, CHIPS)
        near = blocks_ref[:, across].astype(F32)
        beside = blocks_ref[:, 2 + across].astype(F32)
        result[rows, 0:GROUP, :] = jnp.where(core == 0, near, beside).astype(BF16)
        result[rows, GROUP : 2 * GROUP, :] = jnp.where(core == 0, beside, near).astype(BF16)
    copies.append(pltpu.make_async_copy(result, result_ref, result_sem))
    copies[-1].start()
    for copy in copies:
        copy.wait()


def place(where, *arrays):
    grad = jax.ShapeDtypeStruct((D, D), F32)
    rows = jax.ShapeDtypeStruct((ROWS // 8, 8, D), BF16)
    final = len(arrays) > 2
    scratch = [pltpu.VMEM((2, 2, QUARTER, D), F32)]
    if final:
        scratch.append(pltpu.VMEM((ROWS // 8, 8, D), BF16))
    scratch.append(pltpu.SemaphoreType.DMA((2, 2)))
    if final:
        scratch.append(pltpu.SemaphoreType.DMA(()))
    return pl.pallas_call(
        far_kernel if final else near_kernel,
        out_shape=(grad, grad, rows) if final else (grad, grad),
        in_specs=[pl.BlockSpec(memory_space=pltpu.SMEM)]
        + ([VMEM] * 3 + [ANY] * 2 if final else [VMEM] * 2),
        out_specs=(ANY,) * (3 if final else 2),
        scratch_shapes=scratch,
        input_output_aliases={4: 0, 5: 1} if final else {},
        compiler_params=pltpu.CompilerParams(vmem_limit_bytes=16 << 20),
        cost_estimate=pl.CostEstimate(flops=10**6, bytes_accessed=3 << 20, transcendentals=0),
        name="place_far" if final else "place_near",
    )(where, *arrays)


def exchanged(blocks):
    return lax.all_to_all(blocks, FRAME, 0, 0, tiled=True)


def on_device(
    cotangent,
    q_spatial,
    k_spatial,
    v_spatial,
    q_temporal,
    k_temporal,
    v_temporal,
    w_qkv_spatial,
    w_out_spatial,
    w_qkv_temporal,
    w_out_temporal,
):
    core = lax.axis_index("frame_2").astype(jnp.int32)
    chip = lax.axis_index("frame_0").astype(jnp.int32)
    core_of = core.reshape(1)
    where = jnp.stack([core, chip])
    factor = 1.0 / math.sqrt(48 * ROWS)

    def over_core(send, keep):
        got = lax.ppermute(send, "frame_2", SWAP)
        both = keep + got.astype(F32)
        theirs = lax.dynamic_slice_in_dim(both, (1 - chip) * QUARTER, QUARTER, 0).astype(BF16)
        ours = lax.dynamic_slice_in_dim(both, chip * QUARTER, QUARTER, 0)
        got = lax.ppermute(theirs, "frame_0", SWAP)
        return ours, got

    d_x1 = spatial(cotangent, q_spatial, k_spatial, v_spatial, w_out_spatial, w_qkv_spatial)
    d_x1_t = exchanged(d_x1)
    mixed_t, probs_t = attend(q_temporal, k_temporal, v_temporal)
    halves = spatial_grad(q_spatial, k_spatial, v_spatial, cotangent, core_of, factor)
    keep_s, got_s = over_core(*halves)
    parts_t = quarters(mixed_t, d_x1_t, factor)
    parts_t = lax.all_to_all(parts_t, ("frame_0", "frame_2"), 0, 0, tiled=True)
    pieces = fold(keep_s, got_s, parts_t)
    parts = lax.all_to_all(pieces, "frame_1", 0, 0, tiled=True)
    near_r, send_r = temporal(
        chip.reshape(1), d_x1_t, q_temporal, k_temporal, v_temporal, probs_t, w_out_temporal, w_qkv_temporal
    )
    far_r = lax.ppermute(send_r, "frame_0", SWAP)
    total = total_of(parts)
    own = lax.all_to_all(total, "frame_1", 0, 0, tiled=True)
    keep_r, send_r = order(core_of, near_r, far_r)
    got_r = lax.ppermute(send_r, "frame_2", SWAP)
    blocks = jnp.concatenate([keep_r, got_r], axis=1)
    blocks = lax.all_to_all(blocks, "frame_1", 0, 0, tiled=True)
    across = lax.ppermute(own, "frame_0", SWAP)
    beside = lax.ppermute(own, "frame_2", SWAP)
    far = lax.ppermute(across, "frame_2", SWAP)
    grads = place(where, own, beside)
    first, second, result = place(where, across, far, blocks, *grads)
    return (result.reshape(1, ROWS, D), first, second)


def solution(mesh):
    finer = Mesh(
        mesh.devices.reshape(mesh.shape["clip"], 2, 12, 2),
        ("clip", "frame_0", "frame_1", "frame_2"),
    )
    in_specs = (
        P(CLIP_FRAME, None, None),
        P(CLIP_FRAME, None, None),
        P(CLIP_FRAME, None, None),
        P(CLIP_FRAME, None, None),
        P("clip", FRAME, None),
        P("clip", FRAME, None),
        P("clip", FRAME, None),
        P(),
        P(),
        P(),
        P(),
    )
    out_specs = (P(CLIP_FRAME, None, None), P("clip", None), P("clip", None))
    return jax.shard_map(
        on_device, mesh=finer, in_specs=in_specs, out_specs=out_specs, check_vma=False
    )
```

```python
import functools
import math

import jax
import jax.numpy as jnp
from jax import lax
from jax.experimental import pallas as pl
from jax.experimental.pallas import tpu as pltpu
from jax.sharding import Mesh
from jax.sharding import PartitionSpec as P


D = 512
HEADS = 8
ROWS = 192
GROUP = 4
PAIR = 128
PAIRS = D // PAIR
HALF = D // 2
QUARTER = D // 4
CHIPS = 12
BANDS = 3
BAND = 88
LANES = 128
F32 = jnp.float32
BF16 = jnp.bfloat16
NT = (((1,), (1,)), ((), ()))
TN = (((0,), (0,)), ((), ()))
NN = (((1,), (0,)), ((), ()))
FRAME = ("frame_0", "frame_1", "frame_2")
CLIP_FRAME = ("clip", "frame_0", "frame_1", "frame_2")
SCALE = 1.0 / math.sqrt(D // HEADS)
SWAP = [(0, 1), (1, 0)]
VMEM = pl.BlockSpec(memory_space=pltpu.VMEM)
ANY = pl.BlockSpec(memory_space=pl.ANY)


def mm(a, b, dims):
    return lax.dot_general(a, b, dims, preferred_element_type=F32)


def stacked(x, low):
    zero = jnp.zeros_like(x)
    return jnp.concatenate([jnp.where(low, x, zero), jnp.where(low, zero, x)], axis=0)


def joined(x, low):
    return jnp.where(low, x[:ROWS], x[ROWS:])


def softmax_cols(scores, same):
    if same is not None:
        scores = jnp.where(same, scores, -1e30)
    shifted = jnp.exp(scores - jnp.max(scores, axis=0, keepdims=True))
    return shifted * (1.0 / jnp.sum(shifted, axis=0, keepdims=True))


def low_lanes():
    return lax.broadcasted_iota(jnp.int32, (ROWS, PAIR), 1) < D // HEADS


def same_patch():
    rows = lax.broadcasted_iota(jnp.int32, (ROWS, 2 * ROWS), 0)
    cols = lax.broadcasted_iota(jnp.int32, (ROWS, 2 * ROWS), 1)
    return jnp.bitwise_and(rows - cols, GROUP - 1) == 0


def score_back(probs, v, dm2):
    d_probs = mm(v, dm2, NT)
    inner = jnp.sum(probs * d_probs, axis=0, keepdims=True)
    return (probs * (d_probs - inner)).astype(BF16)


def rows_back(p, probs, d_scores, q2, k, dm2, dqkv_ref, low):
    dqkv_ref[:, pl.ds(p * PAIR, PAIR)] = joined(mm(d_scores, k * BF16(SCALE), TN), low).astype(BF16)
    dqkv_ref[:, pl.ds(D + p * PAIR, PAIR)] = mm(d_scores, q2, NN).astype(BF16)
    dqkv_ref[:, pl.ds(2 * D + p * PAIR, PAIR)] = mm(probs.astype(BF16), dm2, NN).astype(BF16)


def spatial_kernel(x_hbm, q_hbm, k_hbm, v_hbm, wo_hbm, wqkv_hbm, out_ref,
                   x_ref, q_ref, k_ref, v_ref, wo_ref, wqkv_ref, dm_ref, dqkv_ref, probs_ref, d_scores_ref, sems):
    pairs = ((q_hbm, q_ref), (k_hbm, k_ref), (x_hbm, x_ref), (wo_hbm, wo_ref), (v_hbm, v_ref), (wqkv_hbm, wqkv_ref))
    copies = [pltpu.make_async_copy(src, dst, sems.at[i]) for i, (src, dst) in enumerate(pairs)]
    for copy in copies:
        copy.start()
    low = low_lanes()

    def queries(p):
        return stacked(q_ref[0, :, pl.ds(p * PAIR, PAIR)] * BF16(SCALE), low)

    for copy in copies[:2]:
        copy.wait()
    for p in range(PAIRS):
        probs_ref[p] = softmax_cols(mm(k_ref[0, :, pl.ds(p * PAIR, PAIR)], queries(p), NT), None)
    for copy in copies[2:4]:
        copy.wait()
    x = x_ref[0]
    dm_ref[...] = mm(x, wo_ref[...], NT).astype(BF16)
    copies[4].wait()
    for p in range(PAIRS):
        cols = pl.ds(p * PAIR, PAIR)
        d_scores_ref[p] = score_back(probs_ref[p], v_ref[0, :, cols], stacked(dm_ref[:, cols], low))
    for p in range(PAIRS):
        cols = pl.ds(p * PAIR, PAIR)
        dm2 = stacked(dm_ref[:, cols], low)
        rows_back(p, probs_ref[p], d_scores_ref[p], queries(p), k_ref[0, :, cols], dm2, dqkv_ref, low)
    copies[5].wait()
    out = x.astype(F32) + mm(dqkv_ref[...], wqkv_ref[...], NT)
    out_ref[...] = out.astype(BF16).reshape(ROWS // GROUP, GROUP, D)


def spatial(x, q, k, v, wo, wqkv):
    rows = pltpu.VMEM((1, ROWS, D), BF16)
    return pl.pallas_call(
        spatial_kernel,
        out_shape=jax.ShapeDtypeStruct((ROWS // GROUP, GROUP, D), BF16),
        in_specs=[ANY] * 6,
        out_specs=VMEM,
        scratch_shapes=[rows] * 4
        + [
            pltpu.VMEM((D, D), BF16),
            pltpu.VMEM((D, 3 * D), BF16),
            pltpu.VMEM((ROWS, D), BF16),
            pltpu.VMEM((ROWS, 3 * D), BF16),
            pltpu.VMEM((PAIRS, ROWS, 2 * ROWS), F32),
            pltpu.VMEM((PAIRS, ROWS, 2 * ROWS), BF16),
            pltpu.SemaphoreType.DMA((6,)),
        ],
        cost_estimate=pl.CostEstimate(flops=8 * 10**8, bytes_accessed=4 << 20, transcendentals=300000),
        name="spatial_back",
    )(x, q, k, v, wo, wqkv)


def spatial_grad_kernel(factor, core_ref, q_ref, k_ref, v_ref, x_ref, send_ref, keep_ref, mixed_ref):
    low = low_lanes()
    for p in range(PAIRS):
        cols = pl.ds(p * PAIR, PAIR)
        q2 = stacked(q_ref[0, :, cols] * BF16(SCALE), low)
        probs = softmax_cols(mm(k_ref[0, :, cols], q2, NT), None)
        mixed_ref[:, cols] = joined(mm(probs.astype(BF16), v_ref[0, :, cols], TN), low).astype(BF16)
    outer_kernel(factor, core_ref, mixed_ref, x_ref, send_ref, keep_ref)


def spatial_grad(q, k, v, x, core, factor):
    return pl.pallas_call(
        functools.partial(spatial_grad_kernel, factor),
        out_shape=(jax.ShapeDtypeStruct((HALF, D), BF16), jax.ShapeDtypeStruct((HALF, D), F32)),
        in_specs=[pl.BlockSpec(memory_space=pltpu.SMEM)] + [VMEM] * 4,
        out_specs=(VMEM, VMEM),
        scratch_shapes=[pltpu.VMEM((ROWS, D), BF16)],
        compiler_params=pltpu.CompilerParams(vmem_limit_bytes=16 << 20),
        cost_estimate=pl.CostEstimate(flops=3 * 10**8, bytes_accessed=2 << 20, transcendentals=300000),
        name="spatial_grad",
    )(core, q, k, v, x)


def flatten(refs, flat_ref, first=0):
    for i, ref in enumerate(refs, first):
        flat_ref[i] = ref[...].reshape(ROWS, D)


def attend_kernel(q_ref, k_ref, v_ref, mixed_ref, probs_ref, flat_ref):
    low, same = low_lanes(), same_patch()
    flatten((q_ref, k_ref, v_ref), flat_ref)
    for p in range(PAIRS):
        cols = pl.ds(p * PAIR, PAIR)
        probs = softmax_cols(mm(flat_ref[1, :, cols], stacked(flat_ref[0, :, cols] * BF16(SCALE), low), NT), same)
        probs_ref[p] = probs
        mixed_ref[:, cols] = joined(mm(probs.astype(BF16), flat_ref[2, :, cols], TN), low).astype(BF16)


def attend(q, k, v):
    return pl.pallas_call(
        attend_kernel,
        out_shape=(
            jax.ShapeDtypeStruct((ROWS, D), BF16),
            jax.ShapeDtypeStruct((PAIRS, ROWS, 2 * ROWS), F32),
        ),
        in_specs=[VMEM] * 3,
        out_specs=(VMEM, VMEM),
        scratch_shapes=[pltpu.VMEM((3, ROWS, D), BF16)],
        compiler_params=pltpu.CompilerParams(vmem_limit_bytes=16 << 20),
        cost_estimate=pl.CostEstimate(flops=2 * 10**8, bytes_accessed=2 << 20, transcendentals=300000),
        name="temporal_attend",
    )(q, k, v)


def temporal_kernel(chip_ref, x_hbm, q_hbm, k_hbm, v_hbm, probs_hbm, wo_hbm, wqkv_hbm, keep_ref, send_ref,
                    x_ref, q_ref, k_ref, v_ref, probs_ref, wo_ref, wqkv_ref, dm_ref, dqkv_ref, flat_ref, block_ref, d_scores_ref, sems):
    pairs = (
        (x_hbm, x_ref), (wo_hbm, wo_ref), (q_hbm, q_ref), (k_hbm, k_ref), (v_hbm, v_ref),
        (probs_hbm, probs_ref), (wqkv_hbm, wqkv_ref),
    )
    copies = [pltpu.make_async_copy(src, dst, sems.at[i]) for i, (src, dst) in enumerate(pairs)]
    for copy in copies:
        copy.start()
    low = low_lanes()
    copies[0].wait()
    flatten((x_ref,), flat_ref)
    x = flat_ref[0]
    copies[1].wait()
    dm_ref[...] = mm(x, wo_ref[...], NT).astype(BF16)
    for copy in copies[2:6]:
        copy.wait()
    flatten((q_ref, k_ref, v_ref), flat_ref, 1)
    for p in range(PAIRS):
        cols = pl.ds(p * PAIR, PAIR)
        d_scores_ref[p] = score_back(probs_ref[p], flat_ref[3, :, cols], stacked(dm_ref[:, cols], low))
    for p in range(PAIRS):
        cols = pl.ds(p * PAIR, PAIR)
        q2 = stacked(flat_ref[1, :, cols] * BF16(SCALE), low)
        dm2 = stacked(dm_ref[:, cols], low)
        rows_back(p, probs_ref[p], d_scores_ref[p], q2, flat_ref[2, :, cols], dm2, dqkv_ref, low)
    copies[6].wait()
    out = x.astype(F32) + mm(dqkv_ref[...], wqkv_ref[...], NT)
    block_ref[...] = out.astype(BF16).reshape(ROWS // GROUP, GROUP, D)
    chip = chip_ref[0]
    keep_ref[...] = block_ref[pl.ds(chip * 2 * CHIPS, 2 * CHIPS)]
    send_ref[...] = block_ref[pl.ds((1 - chip) * 2 * CHIPS, 2 * CHIPS)]


def temporal(chip, x, q, k, v, probs, wo, wqkv):
    rows = pltpu.VMEM((ROWS // GROUP, GROUP, D), BF16)
    half = jax.ShapeDtypeStruct((2 * CHIPS, GROUP, D), BF16)
    return pl.pallas_call(
        temporal_kernel,
        out_shape=(half, half),
        in_specs=[pl.BlockSpec(memory_space=pltpu.SMEM)] + [ANY] * 7,
        out_specs=(VMEM, VMEM),
        scratch_shapes=[rows] * 4
        + [
            pltpu.VMEM((PAIRS, ROWS, 2 * ROWS), F32),
            pltpu.VMEM((D, D), BF16),
            pltpu.VMEM((D, 3 * D), BF16),
            pltpu.VMEM((ROWS, D), BF16),
            pltpu.VMEM((ROWS, 3 * D), BF16),
            pltpu.VMEM((4, ROWS, D), BF16),
            rows,
            pltpu.VMEM((PAIRS, ROWS, 2 * ROWS), BF16),
            pltpu.SemaphoreType.DMA((7,)),
        ],
        cost_estimate=pl.CostEstimate(flops=7 * 10**8, bytes_accessed=5 << 20, transcendentals=0),
        name="temporal_back",
    )(chip, x, q, k, v, probs, wo, wqkv)


def order_kernel(core_ref, near_ref, far_ref, keep_ref, send_ref):
    core = core_ref[0]
    for i, source in enumerate((near_ref, far_ref)):
        keep_ref[:, i : i + 1] = source[:, pl.ds(core, 1)]
        send_ref[:, i : i + 1] = source[:, pl.ds(1 - core, 1)]


def order(core, near, far):
    half = jax.ShapeDtypeStruct((CHIPS, 2, GROUP, D), BF16)
    return pl.pallas_call(
        order_kernel,
        out_shape=(half, half),
        in_specs=[pl.BlockSpec(memory_space=pltpu.SMEM), VMEM, VMEM],
        out_specs=(VMEM, VMEM),
        compiler_params=pltpu.CompilerParams(vmem_limit_bytes=16 << 20),
        cost_estimate=pl.CostEstimate(flops=10**5, bytes_accessed=1 << 19, transcendentals=0),
        name="order",
    )(core, near.reshape(half.shape), far.reshape(half.shape))


def outer_kernel(factor, core_ref, mixed_ref, x_ref, send_ref, keep_ref):
    core = core_ref[0]
    x = x_ref[...].reshape(ROWS, D)
    theirs = pl.ds(pl.multiple_of((1 - core) * HALF, HALF), HALF)
    ours = pl.ds(pl.multiple_of(core * HALF, HALF), HALF)
    send_ref[...] = (mm(mixed_ref[:, theirs], x, TN) * factor).astype(BF16)
    keep_ref[...] = mm(mixed_ref[:, ours], x, TN) * factor


def outer(mixed, x, core, factor):
    return pl.pallas_call(
        functools.partial(outer_kernel, factor),
        out_shape=(jax.ShapeDtypeStruct((HALF, D), BF16), jax.ShapeDtypeStruct((HALF, D), F32)),
        in_specs=[pl.BlockSpec(memory_space=pltpu.SMEM), VMEM, VMEM],
        out_specs=(VMEM, VMEM),
        compiler_params=pltpu.CompilerParams(vmem_limit_bytes=16 << 20),
        cost_estimate=pl.CostEstimate(flops=10**8, bytes_accessed=1 << 20, transcendentals=0),
        name="weight_grad",
    )(core, mixed, x)


def fold_kernel(keep_s_ref, got_s_ref, keep_t_ref, got_t_ref, out_ref, sum_ref):
    sum_ref[0:QUARTER, :] = keep_s_ref[...] + got_s_ref[...].astype(F32)
    sum_ref[QUARTER:HALF, :] = keep_t_ref[...] + got_t_ref[...].astype(F32)
    sum_ref[HALF:, :] = jnp.zeros((BANDS * BAND - HALF, D), F32)
    for band in range(BANDS):
        for j in range(PAIRS):
            out_ref[band * PAIRS + j] = sum_ref[
                band * BAND : (band + 1) * BAND, j * LANES : (j + 1) * LANES
            ].astype(BF16)


def fold(keep_s, got_s, keep_t, got_t):
    return pl.pallas_call(
        fold_kernel,
        out_shape=jax.ShapeDtypeStruct((CHIPS, BAND, LANES), BF16),
        in_specs=[VMEM] * 4,
        out_specs=VMEM,
        scratch_shapes=[pltpu.VMEM((BANDS * BAND, D), F32)],
        compiler_params=pltpu.CompilerParams(vmem_limit_bytes=16 << 20),
        cost_estimate=pl.CostEstimate(flops=10**6, bytes_accessed=1 << 20, transcendentals=0),
        name="fold",
    )(keep_s, got_s, keep_t, got_t)


def total_kernel(parts_ref, out_ref):
    total = parts_ref[0].astype(F32)
    for i in range(1, CHIPS):
        total = total + parts_ref[i].astype(F32)
    total = total.astype(BF16)
    for i in range(CHIPS):
        out_ref[i] = total


def total_of(parts):
    return pl.pallas_call(
        total_kernel,
        out_shape=jax.ShapeDtypeStruct((CHIPS, BAND, LANES), BF16),
        in_specs=[VMEM],
        out_specs=VMEM,
        compiler_params=pltpu.CompilerParams(vmem_limit_bytes=16 << 20),
        cost_estimate=pl.CostEstimate(flops=10**6, bytes_accessed=1 << 19, transcendentals=0),
        name="total",
    )(parts)


def place_quarter(source, c, y, outs, buffer, sems):
    for band in range(BANDS):
        for j in range(PAIRS):
            for g in range(2):
                low = max(band * BAND, g * QUARTER)
                high = min((band + 1) * BAND, (g + 1) * QUARTER)
                if low < high:
                    buffer[g, low - g * QUARTER : high - g * QUARTER, j * LANES : (j + 1) * LANES] = source[
                        band * PAIRS + j, low - band * BAND : high - band * BAND, :
                    ].astype(F32)
    rows = pl.ds(pl.multiple_of(c * HALF + y * QUARTER, QUARTER), QUARTER)
    copies = [pltpu.make_async_copy(buffer.at[g], outs[g].at[rows], sems.at[g]) for g in range(2)]
    for copy in copies:
        copy.start()
    return copies


def near_kernel(where_ref, own_ref, beside_ref, first_ref, second_ref, buffers, sems):
    core, chip = where_ref[0], where_ref[1]
    outs = (first_ref, second_ref)
    copies = place_quarter(own_ref, core, chip, outs, buffers.at[0], sems.at[0])
    copies += place_quarter(beside_ref, 1 - core, chip, outs, buffers.at[1], sems.at[1])
    for copy in copies:
        copy.wait()


def across_kernel(where_ref, across_ref, *refs):
    first_ref, second_ref, buffers, sems = refs[2:]
    core, chip = where_ref[0], where_ref[1]
    copies = place_quarter(across_ref, core, 1 - chip, (first_ref, second_ref), buffers.at[0], sems.at[0])
    for copy in copies:
        copy.wait()


def place_across(where, across, *outs):
    grad = jax.ShapeDtypeStruct((D, D), F32)
    return pl.pallas_call(
        across_kernel,
        out_shape=(grad, grad),
        in_specs=[pl.BlockSpec(memory_space=pltpu.SMEM), VMEM, ANY, ANY],
        out_specs=(ANY, ANY),
        scratch_shapes=[pltpu.VMEM((1, 2, QUARTER, D), F32), pltpu.SemaphoreType.DMA((1, 2))],
        input_output_aliases={2: 0, 3: 1},
        compiler_params=pltpu.CompilerParams(vmem_limit_bytes=16 << 20),
        cost_estimate=pl.CostEstimate(flops=10**6, bytes_accessed=1 << 20, transcendentals=0),
        name="place_across",
    )(where, across, *outs)


def far_kernel(where_ref, far_ref, blocks_ref, *refs):
    first_ref, second_ref, result_ref, buffers, result, sems, result_sem = refs[2:]
    core, chip = where_ref[0], where_ref[1]
    outs = (first_ref, second_ref)
    copies = place_quarter(far_ref, 1 - core, 1 - chip, outs, buffers.at[1], sems.at[1])
    for across in range(2):
        rows = pl.ds((chip + across - 2 * chip * across) * CHIPS, CHIPS)
        near = blocks_ref[:, across].astype(F32)
        beside = blocks_ref[:, 2 + across].astype(F32)
        result[rows, 0:GROUP, :] = jnp.where(core == 0, near, beside).astype(BF16)
        result[rows, GROUP : 2 * GROUP, :] = jnp.where(core == 0, beside, near).astype(BF16)
    copies.append(pltpu.make_async_copy(result, result_ref, result_sem))
    copies[-1].start()
    for copy in copies:
        copy.wait()


def place(where, *arrays):
    grad = jax.ShapeDtypeStruct((D, D), F32)
    rows = jax.ShapeDtypeStruct((ROWS // 8, 8, D), BF16)
    final = len(arrays) > 2
    scratch = [pltpu.VMEM((2, 2, QUARTER, D), F32)]
    if final:
        scratch.append(pltpu.VMEM((ROWS // 8, 8, D), BF16))
    scratch.append(pltpu.SemaphoreType.DMA((2, 2)))
    if final:
        scratch.append(pltpu.SemaphoreType.DMA(()))
    return pl.pallas_call(
        far_kernel if final else near_kernel,
        out_shape=(grad, grad, rows) if final else (grad, grad),
        in_specs=[pl.BlockSpec(memory_space=pltpu.SMEM)]
        + ([VMEM] * 2 + [ANY] * 2 if final else [VMEM] * 2),
        out_specs=(ANY,) * (3 if final else 2),
        scratch_shapes=scratch,
        input_output_aliases={3: 0, 4: 1} if final else {},
        compiler_params=pltpu.CompilerParams(vmem_limit_bytes=16 << 20),
        cost_estimate=pl.CostEstimate(flops=10**6, bytes_accessed=3 << 20, transcendentals=0),
        name="place_far" if final else "place_near",
    )(where, *arrays)


def exchanged(blocks):
    return lax.all_to_all(blocks, FRAME, 0, 0, tiled=True)


def on_device(
    cotangent,
    q_spatial,
    k_spatial,
    v_spatial,
    q_temporal,
    k_temporal,
    v_temporal,
    w_qkv_spatial,
    w_out_spatial,
    w_qkv_temporal,
    w_out_temporal,
):
    core = lax.axis_index("frame_2").astype(jnp.int32)
    chip = lax.axis_index("frame_0").astype(jnp.int32)
    core_of = core.reshape(1)
    where = jnp.stack([core, chip])
    factor = 1.0 / math.sqrt(48 * ROWS)

    def over_core(send, keep):
        got = lax.ppermute(send, "frame_2", SWAP)
        both = keep + got.astype(F32)
        theirs = lax.dynamic_slice_in_dim(both, (1 - chip) * QUARTER, QUARTER, 0).astype(BF16)
        ours = lax.dynamic_slice_in_dim(both, chip * QUARTER, QUARTER, 0)
        got = lax.ppermute(theirs, "frame_0", SWAP)
        return ours, got

    d_x1 = spatial(cotangent, q_spatial, k_spatial, v_spatial, w_out_spatial, w_qkv_spatial)
    d_x1_t = exchanged(d_x1)
    mixed_t, probs_t = attend(q_temporal, k_temporal, v_temporal)
    halves = spatial_grad(q_spatial, k_spatial, v_spatial, cotangent, core_of, factor)
    keep_s, got_s = over_core(*halves)
    halves = outer(mixed_t, d_x1_t, core_of, factor)
    keep_t, got_t = over_core(*halves)
    pieces = fold(keep_s, got_s, keep_t, got_t)
    parts = lax.all_to_all(pieces, "frame_1", 0, 0, tiled=True)
    near_r, send_r = temporal(
        chip.reshape(1), d_x1_t, q_temporal, k_temporal, v_temporal, probs_t, w_out_temporal, w_qkv_temporal
    )
    far_r = lax.ppermute(send_r, "frame_0", SWAP)
    total = total_of(parts)
    own = lax.all_to_all(total, "frame_1", 0, 0, tiled=True)
    keep_r, send_r = order(core_of, near_r, far_r)
    got_r = lax.ppermute(send_r, "frame_2", SWAP)
    blocks = jnp.concatenate([keep_r, got_r], axis=1)
    blocks = lax.all_to_all(blocks, "frame_1", 0, 0, tiled=True)
    across = lax.ppermute(own, "frame_0", SWAP)
    beside = lax.ppermute(own, "frame_2", SWAP)
    far = lax.ppermute(across, "frame_2", SWAP)
    grads = place(where, own, beside)
    grads = place_across(where, across, *grads)
    first, second, result = place(where, far, blocks, *grads)
    return (result.reshape(1, ROWS, D), first, second)


def solution(mesh):
    finer = Mesh(
        mesh.devices.reshape(mesh.shape["clip"], 2, 12, 2),
        ("clip", "frame_0", "frame_1", "frame_2"),
    )
    in_specs = (
        P(CLIP_FRAME, None, None),
        P(CLIP_FRAME, None, None),
        P(CLIP_FRAME, None, None),
        P(CLIP_FRAME, None, None),
        P("clip", FRAME, None),
        P("clip", FRAME, None),
        P("clip", FRAME, None),
        P(),
        P(),
        P(),
        P(),
    )
    out_specs = (P(CLIP_FRAME, None, None), P("clip", None), P("clip", None))
    return jax.shard_map(
        on_device, mesh=finer, in_specs=in_specs, out_specs=out_specs, check_vma=False
    )
```
